128 devices in a mesh: section: 2 (over x_lo), seq: 8 (over y, core), tp: 8 (over z, x_hi).
Axes of the slice: x: 4 (x_hi: 2, x_lo: 2; x = x_hi * 2 + x_lo), y: 4, z: 4, core: 2. Of those that a mesh axis runs over, the one named last changes fastest.
Arguments:
- hidden_image: bfloat16 [2, 1024, 1536], P(None, 'seq'), may hold values from -6 to 6
- hidden_text: bfloat16 [2, 256, 1536], P(None, 'seq'), may hold values from -6 to 6
- latent: float32 [2, 1024, 64], P(None, 'seq'), may hold values from -6 to 6
- timestep: int32 [2], replicated, may hold values from 14 to 27
- text_length: int32 [2], replicated, may hold values from 64 to 154, as said below
- text_keep: int32 [2, 256], replicated, may hold values 0 or 1
- patch_order: int32 [4], replicated, may hold values from 0 to 3, each once
- stale_image_kv: bfloat16 [2, 2, 1024, 2, 1536], P('section', None, 'seq', None, 'tp'), may hold values from -160 to 160
- stale_text_kv: bfloat16 [2, 2, 256, 2, 1536], P('section', None, 'seq', None, 'tp'), may hold values from -6 to 6
- mod_image: float32 [2, 2, 6, 1536], P('section'), may hold values from -3 to 3
- mod_text: float32 [2, 2, 6, 1536], P('section'), may hold values from -3 to 3
- mod_final: float32 [2, 2, 1536], replicated, may hold values from -3 to 3
- qkv_image: bfloat16 [2, 1536, 3, 1536], P('section', None, None, 'tp'), may hold values from -0.15625 to 0.15625
- out_image: bfloat16 [2, 1536, 1536], P('section', 'tp'), may hold values from -0.15625 to 0.15625
- up_image: bfloat16 [2, 1536, 6144], P('section', None, 'tp'), may hold values from -0.15625 to 0.15625
- down_image: bfloat16 [2, 6144, 1536], P('section', 'tp'), may hold values from -0.078125 to 0.078125
- qkv_text: bfloat16 [2, 1536, 3, 1536], P('section', None, None, 'tp'), may hold values from -0.15625 to 0.15625
- out_text: bfloat16 [2, 1536, 1536], P('section', 'tp'), may hold values from -0.15625 to 0.15625
- up_text: bfloat16 [2, 1536, 6144], P('section', None, 'tp'), may hold values from -0.15625 to 0.15625
- down_text: bfloat16 [2, 6144, 1536], P('section', 'tp'), may hold values from -0.078125 to 0.078125
- final_weight: bfloat16 [1536, 64], replicated, may hold values from -0.3125 to 0.3125
Outputs:
- latent_out: float32 [2, 2, 1024, 64], P('section', None, 'seq')
- image_kv_next: bfloat16 [2, 2, 1024, 2, 1536], P('section', None, 'seq', None, 'tp')
- text_kv_next: bfloat16 [2, 2, 256, 2, 1536], P('section', None, 'seq', None, 'tp')
- text_hidden: bfloat16 [2, 2, 256, 1536], P('section', None, 'seq')
The draws below stay inside these ranges and needn't reach their ends.
Inputs may be any that keep to these rules, and one draw needn't show every extreme that they name: `text_length`: some request has exactly 154 text tokens.
All inputs are finite; a program needn't handle non-finite values.
Results may differ from the reference program's by a relative error of at most 0.023.
Values may be sent and summed in bfloat16 or wider, within the bound.
No kernel may reach another device: no remote copies, remote signals or barrier semaphores. Data moves between devices by JAX's collectives and lax.ppermute only.
A program may use at most 128 MiB of HBM per device.

```python
import jax
import jax.numpy as jnp
from jax import lax

D = 1536
HEADS = 24
HD = 64
FF = 6144
CHANNELS = 64
PATCHES = 4
STEPS = 28
REQ = 2
PT = 32
TQ = 8
IMG = 1024
TXT = 256
LIVE_MAX = 154
N_SEQ = 8


def draw_text_length(key, part):
    first_key, second_key = jax.random.split(jax.random.fold_in(key, 11))
    lengths = jax.random.randint(first_key, (REQ,), TXT // 4, LIVE_MAX + 1)
    chosen = jax.random.randint(second_key, (), 0, REQ)
    return jnp.where(jnp.arange(REQ) == chosen, LIVE_MAX, lengths).astype(jnp.int32)


def draw_stale_image_kv(key, part):
    shape = (2, REQ, IMG, 2, D)
    base_key = jax.random.fold_in(jax.random.fold_in(key, 23), 0)
    values = jnp.clip(jax.random.normal(base_key, shape, jnp.float32), -6.0, 6.0)
    return values.astype(jnp.bfloat16)


def place_ends(array, stream_key, low, largest):
    extent = array.shape
    index_at = [jax.random.randint(jax.random.fold_in(stream_key, axis), (), 0, extent[axis]) for axis in range(len(extent))]
    array = array.at[tuple(index_at)].set(low)
    longest = extent.index(max(extent))
    index_at[longest] = (index_at[longest] + 1) % extent[longest]
    return array.at[tuple(index_at)].set(largest)


def block_levels(stream_key, shape, cuts, least, high):
    level, own = 1.0, jax.random.fold_in(stream_key, 6)
    for axis_at, parts in cuts:
        heights = jnp.exp(jax.random.uniform(jax.random.fold_in(own, axis_at), (parts,), jnp.float32, least / len(cuts), high / len(cuts)))
        level = level * jnp.repeat(heights, shape[axis_at] // parts).reshape([-1 if axis == axis_at else 1 for axis in range(len(shape))])
    return level


def normal_values(rng, extent, scale, limit, cuts=(), held_as=jnp.bfloat16):
    entries = jax.random.normal(rng, extent, jnp.float32) * scale
    if len(cuts) > 0:
        entries = block_levels(rng, extent, cuts, -0.22, 0.18) * entries
    return jnp.clip(entries, min=-limit, max=limit).astype(held_as)


def setup_inputs(seed: int = 0) -> dict:
    key_of = jax.random.split(jax.random.key(seed), 22)
    return {
        "hidden_image": normal_values(key_of[0], (REQ, IMG, D), 1.0, 6.0, ((1, 8),)),
        "hidden_text": normal_values(key_of[1], (REQ, TXT, D), 1.0, 6.0, ((1, 8),)),
        "latent": normal_values(key_of[2], (REQ, IMG, CHANNELS), 1.0, 6.0, ((1, 8),), jnp.float32),
        "timestep": jax.random.randint(key_of[3], (REQ,), STEPS // 2, STEPS).astype(jnp.int32),
        "text_length": draw_text_length(jax.random.fold_in(key_of[21], 71), 0),
        "text_keep": place_ends((jax.random.randint(key_of[5], (REQ, TXT), 0, 2) < 1).astype(jnp.int32), jax.random.fold_in(key_of[5], 1), 0, 1),
        "patch_order": jax.random.permutation(key_of[6], PATCHES).astype(jnp.int32),
        "stale_image_kv": draw_stale_image_kv(jax.random.fold_in(key_of[21], 71), 0),
        "stale_text_kv": normal_values(key_of[8], (2, REQ, TXT, 2, D), 1.0, 6.0, ((0, 2), (2, 8), (4, 8))),
        "mod_image": normal_values(key_of[9], (2, REQ, 6, D), 0.5, 3.0, ((0, 2),), jnp.float32),
        "mod_text": normal_values(key_of[10], (2, REQ, 6, D), 0.5, 3.0, ((0, 2),), jnp.float32),
        "mod_final": normal_values(key_of[11], (REQ, 2, D), 0.5, 3.0, (), jnp.float32),
        "qkv_image": normal_values(key_of[12], (2, D, 3, D), D ** -0.5, 0.15625, ((0, 2), (3, 8))),
        "out_image": normal_values(key_of[13], (2, D, D), D ** -0.5, 0.15625, ((0, 2), (1, 8))),
        "up_image": normal_values(key_of[14], (2, D, FF), D ** -0.5, 0.15625, ((0, 2), (2, 8))),
        "down_image": normal_values(key_of[15], (2, FF, D), FF ** -0.5, 0.078125, ((0, 2), (1, 8))),
        "qkv_text": normal_values(key_of[16], (2, D, 3, D), D ** -0.5, 0.15625, ((0, 2), (3, 8))),
        "out_text": normal_values(key_of[17], (2, D, D), D ** -0.5, 0.15625, ((0, 2), (1, 8))),
        "up_text": normal_values(key_of[18], (2, D, FF), D ** -0.5, 0.15625, ((0, 2), (2, 8))),
        "down_text": normal_values(key_of[19], (2, FF, D), FF ** -0.5, 0.078125, ((0, 2), (1, 8))),
        "final_weight": normal_values(key_of[20], (D, CHANNELS), (D // 4) ** -0.5, 0.3125),
    }


EPSILON = 1e-06
NEGATIVE = -1e+30
TIME_SHIFT = 3.0

def rounded(values):
    return lax.optimization_barrier(values.astype(jnp.bfloat16)).astype(jnp.float32)

def modulate(values, shift_vec, scale_vec):
    mean_value = lax.optimization_barrier(jnp.mean(values, axis=-1, keepdims=True))
    centred = values - mean_value
    variance = lax.optimization_barrier(jnp.mean(centred * centred, axis=-1, keepdims=True))
    normed = centred * lax.rsqrt(variance + EPSILON)
    return normed * (1.0 + scale_vec[:, None, :]) + shift_vec[:, None, :]

def matmul_rows(rows, weight):
    flattened = rows.reshape(-1, rows.shape[-1])
    result = jnp.dot(flattened, weight, preferred_element_type=jnp.float32)
    return result.reshape(rows.shape[:-1] + (weight.shape[-1],))

def project(rows, modulation, weight):
    normed = modulate(rows.astype(jnp.float32), modulation[:, 0], modulation[:, 1]).astype(jnp.bfloat16)
    mixed = matmul_rows(normed, weight.reshape(weight.shape[0], -1)).astype(jnp.bfloat16)
    return mixed.reshape(rows.shape[0], rows.shape[1], 3, -1)

def finish(rows, attended, modulation, out_weight, up_weight, down_weight):
    attention = matmul_rows(attended, out_weight)
    after_attention = rows.astype(jnp.float32) + modulation[:, 2][:, None, :] * attention
    normed = modulate(after_attention, modulation[:, 3], modulation[:, 4]).astype(jnp.bfloat16)
    hidden = jax.nn.gelu(matmul_rows(normed, up_weight), approximate=True).astype(jnp.bfloat16)
    result = after_attention + modulation[:, 5][:, None, :] * matmul_rows(hidden, down_weight)
    return result.astype(jnp.bfloat16)

def attend(queries, keys_all, values_all, key_mask):
    requests = queries.shape[0]
    query_count = queries.shape[1]
    query_heads = queries.reshape(requests, query_count, HEADS, HD).astype(jnp.float32)
    key_heads = keys_all.reshape(requests, keys_all.shape[1], HEADS, HD).astype(jnp.float32)
    value_heads = values_all.reshape(requests, values_all.shape[1], HEADS, HD).astype(jnp.float32)
    scores = jnp.einsum('rqhe,rkhe->rhqk', query_heads, key_heads) * HD ** (-0.5)
    scores = jnp.where(key_mask[:, None, None, :], scores, NEGATIVE)
    rowmax = lax.optimization_barrier(jnp.max(scores, axis=-1, keepdims=True))
    exponent = jnp.where(key_mask[:, None, None, :], jnp.exp(scores - rowmax), 0.0)
    totals = lax.optimization_barrier(jnp.sum(exponent, axis=-1))
    summed = jnp.einsum('rhqk,rkhe->rhqe', rounded(exponent), value_heads)
    result = summed / totals[..., None]
    return jnp.transpose(result, (0, 2, 1, 3)).reshape(requests, query_count, HEADS * HD).astype(jnp.bfloat16)

def sigma_of(index_value):
    progress = 1.0 - index_value / STEPS
    return TIME_SHIFT * progress / (1.0 + (TIME_SHIFT - 1.0) * progress)

def reference(hidden_image, hidden_text, latent, timestep, text_length, text_keep, patch_order, stale_image_kv, stale_text_kv, mod_image, mod_text, mod_final, qkv_image, out_image, up_image, down_image, qkv_text, out_text, up_text, down_text, final_weight):
    positions = jnp.arange(TXT, dtype=jnp.int32)
    valid_text = (positions[None, :] < text_length[:, None]) & (text_keep == 1)
    valid_all = jnp.concatenate([jnp.ones((REQ, IMG), jnp.bool_), valid_text], axis=1)
    image_rows = hidden_image.reshape(REQ, N_SEQ, PATCHES, PT, D)
    text_rows = hidden_text.reshape(REQ, N_SEQ, PATCHES, TQ, D)
    image_kv_list = []
    text_kv_list = []
    text_hidden_list = []
    for layer_index in range(2):
        image_buffer = stale_image_kv[layer_index].reshape(REQ, N_SEQ, PATCHES, PT, 2, D)
        text_buffer = stale_text_kv[layer_index].reshape(REQ, N_SEQ, PATCHES, TQ, 2, D)
        image_result = jnp.zeros_like(image_rows)
        text_result = jnp.zeros_like(text_rows)
        for slot_index in range(PATCHES):
            patch_index = patch_order[slot_index]
            own_image = lax.dynamic_index_in_dim(image_rows, patch_index, 2, keepdims=False).reshape(REQ, N_SEQ * PT, D)
            own_text = text_rows[:, :, slot_index].reshape(REQ, N_SEQ * TQ, D)
            image_qkv = project(own_image, mod_image[layer_index], qkv_image[layer_index])
            text_qkv = project(own_text, mod_text[layer_index], qkv_text[layer_index])
            image_buffer = lax.dynamic_update_index_in_dim(image_buffer, image_qkv[:, :, 1:].reshape(REQ, N_SEQ, PT, 2, D), patch_index, 2)
            text_buffer = text_buffer.at[:, :, slot_index].set(text_qkv[:, :, 1:].reshape(REQ, N_SEQ, TQ, 2, D))
            keys_all = jnp.concatenate([image_buffer.reshape(REQ, IMG, 2, D), text_buffer.reshape(REQ, TXT, 2, D)], axis=1)
            queries = jnp.concatenate([image_qkv[:, :, 0], text_qkv[:, :, 0]], axis=1)
            attended = attend(queries, keys_all[:, :, 0], keys_all[:, :, 1], valid_all)
            image_new = finish(own_image, attended[:, :N_SEQ * PT], mod_image[layer_index], out_image[layer_index], up_image[layer_index], down_image[layer_index])
            text_new = finish(own_text, attended[:, N_SEQ * PT:], mod_text[layer_index], out_text[layer_index], up_text[layer_index], down_text[layer_index])
            image_result = lax.dynamic_update_index_in_dim(image_result, image_new.reshape(REQ, N_SEQ, PT, D), patch_index, 2)
            text_result = text_result.at[:, :, slot_index].set(text_new.reshape(REQ, N_SEQ, TQ, D))
        image_kv_list.append(image_buffer.reshape(REQ, IMG, 2, D))
        text_kv_list.append(text_buffer.reshape(REQ, TXT, 2, D))
        text_hidden_list.append(text_result.reshape(REQ, TXT, D))
        image_rows = image_result
        text_rows = text_result
    final_rows = modulate(image_rows.reshape(REQ, IMG, D).astype(jnp.float32), mod_final[:, 0], mod_final[:, 1]).astype(jnp.bfloat16)
    velocity = matmul_rows(final_rows, final_weight)
    index_value = timestep.astype(jnp.float32)
    sigma_now = sigma_of(index_value)
    sigma_next = sigma_of(index_value + 1.0)
    next_latent = latent + (sigma_next - sigma_now)[:, None, None] * velocity
    denoised = latent - sigma_now[:, None, None] * velocity
    return (jnp.stack([next_latent, denoised]), jnp.stack(image_kv_list), jnp.stack(text_kv_list), jnp.stack(text_hidden_list))
```

```python
import jax
import jax.numpy as jnp
from jax import lax
from jax.experimental import pallas as pl
from jax.experimental.pallas import tpu as pltpu
from jax.sharding import PartitionSpec as P

HD = 64
STEPS = 28
EPSILON = 1e-06
NEGATIVE = -1e30
TIME_SHIFT = 3.0

F32 = jnp.float32
BF16 = jnp.bfloat16

REQ, SLOTS, PT, TQ = 2, 4, 32, 8
ROWS = PT + TQ
CHUNKS = REQ * SLOTS
Z, X = 4, 2
Y, C = 4, 2
RING = (1, 3, 2)
PIECES = ((0, 0), (0, 1), (1, 0), (1, 1), (3, 0), (3, 1), (2, 0), (2, 1))

VMEM = pl.BlockSpec(memory_space=pltpu.VMEM)
SMEM = pl.BlockSpec(memory_space=pltpu.SMEM)


def call(body, name, in_specs, out_shapes, scratch=()):
    return pl.pallas_call(
        body,
        name=name,
        in_specs=list(in_specs),
        out_specs=[VMEM] * len(out_shapes),
        out_shape=[jax.ShapeDtypeStruct(*each) for each in out_shapes],
        scratch_shapes=list(scratch),
        compiler_params=pltpu.CompilerParams(vmem_limit_bytes=40 * 1024 * 1024),
    )


def along_z(value, step):
    pairs = [(z * X + x, (z + step) % Z * X + x) for z in range(Z) for x in range(X)]
    return lax.ppermute(value, "tp", pairs)


def across_x(value):
    return lax.ppermute(value, "tp", [(i, i ^ 1) for i in range(Z * X)])


def along_y(value, step):
    pairs = [(y * C + c, (y + step) % Y * C + c) for y in range(Y) for c in range(C)]
    return lax.ppermute(value, "seq", pairs)


def across_core(value):
    return lax.ppermute(value, "seq", [(i, i ^ 1) for i in range(Y * C)])


def to_next_section(value, flip):
    size = Z * X
    return lax.ppermute(value, ("section", "tp"), [(i, size + (i ^ flip)) for i in range(size)])


def gathered_seq(value):
    far = {(0, 0): value, (0, 1): across_core(value)}
    for step in RING:
        far[step, 0] = along_y(value, step)
    for step in RING:
        far[step, 1] = across_core(far[step, 0])
    return [far[piece] for piece in PIECES]


def spread_z(pair):
    received = {step: along_z(pair, step) for step in RING}
    return [pair] + [received[step] for step in (1, 2, 3)]


def reduced_z(pieces):
    received = [along_z(pieces[step], step) for step in RING]
    return [pieces[0]] + received


def normed(rows, shift, scale):
    mean_value = jnp.mean(rows, axis=-1, keepdims=True)
    centred = rows - mean_value
    variance = jnp.mean(centred * centred, axis=-1, keepdims=True)
    return centred * lax.rsqrt(variance + EPSILON) * (1.0 + scale) + shift


def mm(left, right):
    return jnp.dot(left, right, preferred_element_type=F32)


def store_rows(ref, column, image, text):
    width = image.shape[-1]
    ref[:, 0:PT, column : column + width] = image.reshape(CHUNKS, PT, width).astype(ref.dtype)
    ref[:, PT:ROWS, column : column + width] = text.reshape(CHUNKS, TQ, width).astype(ref.dtype)


def project_all(image_rows, text_rows, weights, q_ref, kv_ref):
    wq_image, wkv_image, wq_text, wkv_text = weights
    image = image_rows[...]
    text = text_rows[...].astype(BF16)
    store_rows(q_ref, 0, mm(image, wq_image[...]), mm(text, wq_text[...]))
    store_rows(kv_ref, 0, mm(image, wkv_image[...]), mm(text, wkv_text[...]))


def project_first(order, image, text, mod_image, mod_text, *refs):
    weights, (q_ref, kv_ref, image_rows, text_rows) = refs[:4], refs[4:]
    for r in range(REQ):
        for k in range(SLOTS):
            rows = image[r, order[k]].astype(F32)
            at = (r * SLOTS + k) * PT
            image_rows[at : at + PT, :] = normed(
                rows, mod_image[r, 0:1], mod_image[r, 1:2]
            ).astype(BF16)
        span = SLOTS * TQ
        text_rows[r * span : (r + 1) * span, :] = normed(
            text[r].astype(F32), mod_text[r, 0:1], mod_text[r, 1:2]
        )
    project_all(image_rows, text_rows, weights, q_ref, kv_ref)


def project_next(place, p0, p1, p2, p3, mod_image, mod_text, *refs):
    weights, (q_ref, kv_ref, image_rows, text_rows) = refs[:4], refs[4:]
    z, x = place[0], place[1]
    for step, piece in enumerate((p0, p1, p2, p3)):
        for flip in range(X):
            from_z = (z + Z - step) % Z
            chunk = from_z * X + (x + flip) % X
            r = chunk // SLOTS
            image_rows[pl.ds(pl.multiple_of(chunk * PT, PT), PT), :] = normed(
                piece[flip, 0:PT, :].astype(F32), mod_image[r, 0:1], mod_image[r, 1:2]
            ).astype(BF16)
            text_rows[pl.ds(pl.multiple_of(chunk * TQ, TQ), TQ), :] = normed(
                piece[flip, PT:ROWS, :].astype(F32), mod_text[r, 0:1], mod_text[r, 1:2]
            )
    project_all(image_rows, text_rows, weights, q_ref, kv_ref)


def attend(place, bias, q_ref, *refs):
    fresh, stale = refs[0:8], refs[8:16]
    out_image, out_text = refs[16:18]
    outs = refs[18:22]
    keys, values, o_image, o_text = refs[22:]
    z, x = place[0], place[1]
    width = q_ref.shape[2]
    heads = width // HD
    image_span = len(fresh) * PT
    text_span = len(fresh) * TQ
    text_from = SLOTS * image_span
    lane_head = lax.broadcasted_iota(jnp.int32, (ROWS, width), 1) // HD

    def fill(r, k, pieces, chunk):
        for d, piece in enumerate(pieces):
            at = k * image_span + d * PT
            keys[r, at : at + PT, :] = piece[chunk, 0:PT, 0:width]
            values[r, at : at + PT, :] = piece[chunk, 0:PT, width:]
        rows = jnp.concatenate([piece[chunk, PT:ROWS, :].astype(F32) for piece in pieces], axis=0)
        at = text_from + k * text_span
        keys[r, at : at + text_span, :] = rows[:, 0:width].astype(BF16)
        values[r, at : at + text_span, :] = rows[:, width:].astype(BF16)

    for r in range(REQ):
        for k in range(1, SLOTS):
            fill(r, k, stale, r * (SLOTS - 1) + k - 1)
    for k in range(SLOTS):
        for r in range(REQ):
            chunk = r * SLOTS + k
            fill(r, k, fresh, chunk)
            rows = q_ref[chunk].astype(F32)
            queries = jnp.concatenate(
                [jnp.where(lane_head == h, rows, 0.0) for h in range(heads)], axis=0
            ).astype(BF16)
            scores = lax.dot_general(
                queries, keys[r], (((1,), (1,)), ((), ())), preferred_element_type=F32
            ) * HD ** (-0.5)
            scores = scores + bias[r : r + 1, :]
            top = jnp.max(scores, axis=-1, keepdims=True)
            weights = jnp.exp(scores - top)
            total = jnp.sum(weights, axis=-1, keepdims=True)
            summed = mm(weights.astype(BF16), values[r]) / total
            merged = jnp.zeros((ROWS, width), F32)
            for h in range(heads):
                merged = jnp.where(lane_head == h, summed[h * ROWS : (h + 1) * ROWS], merged)
            own_z, own_x = chunk // X, chunk % X
            at = (own_z + Z - z) % Z * X + (own_x + x) % X
            o_image[pl.ds(pl.multiple_of(at * PT, PT), PT), :] = merged[0:PT].astype(BF16)
            o_text[pl.ds(pl.multiple_of(at * TQ, TQ), TQ), :] = merged[PT:ROWS]
    image = mm(o_image[...], out_image[...])
    text = mm(o_text[...].astype(BF16), out_text[...])
    store_pieces(outs, image, text)


def store_pieces(outs, image, text):
    width = image.shape[-1]
    for d, out in enumerate(outs):
        rows = image[d * X * PT : (d + 1) * X * PT]
        out[:, 0:PT, :] = rows.reshape(X, PT, width).astype(BF16)
        rows = text[d * X * TQ : (d + 1) * X * TQ]
        out[:, PT:ROWS, :] = rows.reshape(X, TQ, width).astype(BF16)


def add_pieces(p0, p1, p2, p3, keep, send):
    keep[...] = sum(p[0].astype(F32) for p in (p0, p1, p2, p3))
    send[...] = sum(p[1].astype(F32) for p in (p0, p1, p2, p3)).astype(BF16)


def after_attention(rows, keep, received, mod_image, mod_text, h1, b):
    summed = keep[...] + received[...].astype(F32)
    for low, high, mod in ((0, PT, mod_image), (PT, ROWS, mod_text)):
        first = rows[low:high, :].astype(F32) + mod[2:3] * summed[low:high]
        h1[low:high, :] = first
        b[low:high, :] = normed(first, mod[3:4], mod[4:5]).astype(BF16)


def feed_forward(p0, p1, p2, p3, up_image, down_image, up_text, down_text, *refs):
    outs, (image_rows, text_rows) = refs[:4], refs[4:]
    for d, piece in enumerate((p0, p1, p2, p3)):
        for flip in range(X):
            at = d * X + flip
            image_rows[at * PT : (at + 1) * PT, :] = piece[flip, 0:PT, :]
            text_rows[at * TQ : (at + 1) * TQ, :] = piece[flip, PT:ROWS, :].astype(F32)
    hidden = jax.nn.gelu(mm(image_rows[...], up_image[...]), approximate=True).astype(BF16)
    image = mm(hidden, down_image[...])
    hidden = jax.nn.gelu(
        mm(text_rows[...].astype(BF16), up_text[...]), approximate=True
    ).astype(BF16)
    text = mm(hidden, down_text[...])
    store_pieces([outs[(Z - d) % Z] for d in range(Z)], image, text)


def layer_rows(h1, keep, received, mod_image, mod_text):
    summed = keep[...] + received[...].astype(F32)
    image = (h1[0:PT, :] + mod_image[5:6] * summed[0:PT]).astype(BF16)
    text = (h1[PT:ROWS, :] + mod_text[5:6] * summed[PT:ROWS]).astype(BF16)
    return image, text


def after_mlp(h1, keep, received, mod_image, mod_text, y):
    image, text = layer_rows(h1, keep, received, mod_image, mod_text)
    y[0:PT, :] = image
    y[PT:ROWS, :] = text


def last_rows(section, h1, keep, received, mod_image, mod_text, mod_final, weight, first, out):
    image, text = layer_rows(h1, keep, received, mod_image, mod_text)
    rows = normed(image.astype(F32), mod_final[0:1], mod_final[1:2]).astype(BF16)
    velocity = mm(rows, weight[...])
    width = text.shape[-1]
    text = jnp.where(section[0] == 0, first[PT:ROWS, :].astype(F32), text.astype(F32))
    out[:, 0:width] = text.astype(BF16)
    out[:, width:] = jnp.concatenate(
        [velocity[i * TQ : (i + 1) * TQ] for i in range(PT // TQ)], axis=1
    ).astype(BF16)


def outputs(section, order, factor, received, latent, latent_out, text_out):
    width = text_out.shape[-1]
    channels = latent.shape[-1]
    count = section[0] * CHUNKS
    for r in range(REQ):
        for k in range(SLOTS):
            chunk = r * SLOTS + k
            text_out[chunk] = received[count + chunk, :, 0:width]
            rows = received[CHUNKS + chunk, :, width:].astype(F32)
            velocity = jnp.concatenate(
                [rows[:, i * channels : (i + 1) * channels] for i in range(PT // TQ)], axis=0
            )
            latent_out[r, order[k]] = latent[r, order[k]] + factor[r] * velocity


def sigma_of(index_value):
    progress = 1.0 - index_value / STEPS
    return TIME_SHIFT * progress / (1.0 + (TIME_SHIFT - 1.0) * progress)


def on_device(
    hidden_image,
    hidden_text,
    latent,
    timestep,
    text_length,
    text_keep,
    patch_order,
    stale_image_kv,
    stale_text_kv,
    mod_image,
    mod_text,
    mod_final,
    qkv_image,
    out_image,
    up_image,
    down_image,
    qkv_text,
    out_text,
    up_text,
    down_text,
    final_weight,
):
    d_model = hidden_image.shape[2]
    width = qkv_image.shape[3]
    section = lax.axis_index("section")
    tp = lax.axis_index("tp")
    seq = lax.axis_index("seq")
    own_r, own_k = tp // SLOTS, tp % SLOTS
    place = jnp.stack([tp // X, tp % X]).astype(jnp.int32)
    section_ref = section.astype(jnp.int32)[None]
    inverse = jnp.zeros((SLOTS,), jnp.int32).at[patch_order].set(jnp.arange(SLOTS, dtype=jnp.int32))

    stale_image = stale_image_kv[0].reshape(REQ, SLOTS, PT, 2 * width)
    stale_text = stale_text_kv[0].reshape(REQ, SLOTS, TQ, 2 * width)
    stale = jnp.concatenate(
        [
            jnp.concatenate(
                [
                    lax.dynamic_index_in_dim(stale_image, patch_order[k], 1, keepdims=True)
                    for k in range(1, SLOTS)
                ],
                axis=1,
            ),
            stale_text[:, 1:],
        ],
        axis=2,
    ).reshape(REQ * (SLOTS - 1), ROWS, 2 * width)
    stale_pieces = gathered_seq(stale)

    positions = jnp.arange(text_keep.shape[1], dtype=jnp.int32)
    valid = (positions[None, :] < text_length[:, None]) & (text_keep == 1)
    text_bias = jnp.where(valid, 0.0, NEGATIVE).astype(F32).reshape(REQ, Y * C, SLOTS, TQ)
    piece_seq = [(seq // C + Y - step) % Y * C + (seq + flip) % C for step, flip in PIECES]
    text_bias = jnp.stack(
        [lax.dynamic_index_in_dim(text_bias, each, 1, keepdims=False) for each in piece_seq], axis=2
    )
    bias = jnp.concatenate(
        [jnp.zeros((REQ, Y * C * SLOTS * PT), F32), text_bias.reshape(REQ, -1)], axis=1
    )

    def split_qkv(weight):
        return weight[0, :, 0], weight[0, :, 1:].reshape(d_model, 2 * width)

    weights = split_qkv(qkv_image) + split_qkv(qkv_text)
    own_mod_image = lax.dynamic_index_in_dim(mod_image[0], own_r, 0, keepdims=False)
    own_mod_text = lax.dynamic_index_in_dim(mod_text[0], own_r, 0, keepdims=False)
    own_mod_final = lax.dynamic_index_in_dim(mod_final, own_r, 0, keepdims=False)

    image_in = hidden_image.reshape(REQ, SLOTS, PT, d_model)
    own_rows = jnp.concatenate(
        [
            lax.dynamic_slice(
                image_in, (own_r, patch_order[own_k], 0, 0), (1, 1, PT, d_model)
            ).reshape(PT, d_model),
            lax.dynamic_slice(
                hidden_text, (own_r, own_k * TQ, 0), (1, TQ, d_model)
            ).reshape(TQ, d_model),
        ],
        axis=0,
    )

    qkv_shapes = [((CHUNKS, ROWS, width), BF16), ((CHUNKS, ROWS, 2 * width), BF16)]
    qkv_scratch = [
        pltpu.VMEM((CHUNKS * PT, d_model), BF16),
        pltpu.VMEM((CHUNKS * TQ, d_model), F32),
    ]
    piece = ((X, ROWS, d_model), BF16)
    row_f32, row_bf16 = ((ROWS, d_model), F32), ((ROWS, d_model), BF16)
    key_count = Y * C * SLOTS * ROWS

    def reduced(pieces):
        keep, send = call(add_pieces, "add_pieces", [VMEM] * 4, [row_f32, row_bf16])(
            *reduced_z(pieces)
        )
        return keep, across_x(send)

    def rest_of_layer(q, kv, rows):
        partial = call(
            attend,
            "attend",
            [SMEM] + [VMEM] * 20,
            [piece] * 4,
            [
                pltpu.VMEM((REQ, key_count, width), BF16),
                pltpu.VMEM((REQ, key_count, width), BF16),
                pltpu.VMEM((CHUNKS * PT, width), BF16),
                pltpu.VMEM((CHUNKS * TQ, width), F32),
            ],
        )(place, bias, q, *gathered_seq(kv), *stale_pieces, out_image[0], out_text[0])
        keep, received = reduced(partial)
        h1, b = call(after_attention, "after_attention", [VMEM] * 5, [row_f32, row_bf16])(
            rows, keep, received, own_mod_image, own_mod_text
        )
        pieces = spread_z(jnp.stack([b, across_x(b)]))
        partial = call(feed_forward, "feed_forward", [VMEM] * 8, [piece] * 4, qkv_scratch)(
            *pieces, up_image[0], down_image[0], up_text[0], down_text[0]
        )
        keep, received = reduced(partial)
        return h1, keep, received

    q, kv_first = call(
        project_first, "project_first", [SMEM] + [VMEM] * 8, qkv_shapes, qkv_scratch
    )(
        patch_order,
        image_in,
        hidden_text,
        mod_image[0],
        mod_text[0],
        *weights,
    )
    h1, keep, received = rest_of_layer(q, kv_first, own_rows)
    (y_first,) = call(after_mlp, "after_mlp", [VMEM] * 5, [row_bf16])(
        h1, keep, received, own_mod_image, own_mod_text
    )
    arrived = to_next_section(y_first, 0)
    pieces = spread_z(jnp.stack([arrived, to_next_section(y_first, 1)]))
    q, kv_next = call(
        project_next, "project_next", [SMEM] + [VMEM] * 10, qkv_shapes, qkv_scratch
    )(place, *pieces, mod_image[0], mod_text[0], *weights)
    h1, keep, received = rest_of_layer(q, kv_next, arrived)
    channels = final_weight.shape[1]
    packed_width = d_model + PT // TQ * channels
    (packed,) = call(
        last_rows, "last_rows", [SMEM] + [VMEM] * 8, [((TQ, packed_width), BF16)]
    )(
        section_ref,
        h1,
        keep,
        received,
        own_mod_image,
        own_mod_text,
        own_mod_final,
        final_weight,
        y_first,
    )
    group = 2 * CHUNKS
    shared = lax.all_to_all(
        jnp.broadcast_to(packed[None], (group,) + packed.shape), ("section", "tp"), 0, 0, tiled=True
    )
    index_value = timestep.astype(F32)
    sigma_now = sigma_of(index_value)
    sigma_next = sigma_of(index_value + 1.0)
    factor = jnp.where(section == 0, sigma_next - sigma_now, -sigma_now)
    latent_part, text_hidden = call(
        outputs,
        "outputs",
        [SMEM] * 3 + [VMEM] * 2,
        [((REQ, SLOTS, PT, channels), F32), ((CHUNKS, TQ, d_model), BF16)],
    )(
        section_ref,
        patch_order,
        factor,
        shared,
        latent.reshape(REQ, SLOTS, PT, channels),
    )
    kv = jnp.where(section == 0, kv_first, kv_next).reshape(REQ, SLOTS, ROWS, 2, width)
    image_kv = jnp.concatenate(
        [
            lax.dynamic_index_in_dim(kv[:, :, :PT], inverse[p], 1, keepdims=True)
            for p in range(SLOTS)
        ],
        axis=1,
    )
    return (
        latent_part.reshape(1, REQ, SLOTS * PT, channels),
        image_kv.reshape(1, REQ, SLOTS * PT, 2, width),
        kv[:, :, PT:].reshape(1, REQ, SLOTS * TQ, 2, width),
        text_hidden.reshape(1, REQ, SLOTS * TQ, d_model),
    )


def solution(mesh):
    in_specs = (
        P(None, "seq", None),
        P(None, "seq", None),
        P(None, "seq", None),
        P(),
        P(),
        P(),
        P(),
        P("section", None, "seq", None, "tp"),
        P("section", None, "seq", None, "tp"),
        P("section", None, None, None),
        P("section", None, None, None),
        P(),
        P("section", None, None, "tp"),
        P("section", "tp", None),
        P("section", None, "tp"),
        P("section", "tp", None),
        P("section", None, None, "tp"),
        P("section", "tp", None),
        P("section", None, "tp"),
        P("section", "tp", None),
        P(),
    )
    out_specs = (
        P("section", None, "seq", None),
        P("section", None, "seq", None, "tp"),
        P("section", None, "seq", None, "tp"),
        P("section", None, "seq", None),
    )
    return jax.shard_map(
        on_device, mesh=mesh, in_specs=in_specs, out_specs=out_specs, check_vma=False
    )
```

```python
import jax
import jax.numpy as jnp
from jax import lax
from jax.experimental import pallas as pl
from jax.experimental.pallas import tpu as pltpu
from jax.sharding import PartitionSpec as P

HD = 64
STEPS = 28
EPSILON = 1e-06
NEGATIVE = -1e30
TIME_SHIFT = 3.0

F32 = jnp.float32
BF16 = jnp.bfloat16

REQ, SLOTS, PT, TQ = 2, 4, 32, 8
ROWS = PT + TQ
CHUNKS = REQ * SLOTS
Z, X = 4, 2
Y, C = 4, 2
LANES = 128
RING = (1, 3, 2)
PIECES = ((0, 0), (0, 1), (1, 0), (1, 1), (3, 0), (3, 1), (2, 0), (2, 1))

VMEM = pl.BlockSpec(memory_space=pltpu.VMEM)
SMEM = pl.BlockSpec(memory_space=pltpu.SMEM)


def call(body, name, in_specs, out_shapes, scratch=()):
    return pl.pallas_call(
        body,
        name=name,
        in_specs=list(in_specs),
        out_specs=[VMEM] * len(out_shapes),
        out_shape=[jax.ShapeDtypeStruct(*each) for each in out_shapes],
        scratch_shapes=list(scratch),
        compiler_params=pltpu.CompilerParams(vmem_limit_bytes=40 * 1024 * 1024),
    )


def along_z(value, step):
    pairs = [(z * X + x, (z + step) % Z * X + x) for z in range(Z) for x in range(X)]
    return lax.ppermute(value, "tp", pairs)


def across_x(value):
    return lax.ppermute(value, "tp", [(i, i ^ 1) for i in range(Z * X)])


def along_y(value, step):
    pairs = [(y * C + c, (y + step) % Y * C + c) for y in range(Y) for c in range(C)]
    return lax.ppermute(value, "seq", pairs)


def across_core(value):
    return lax.ppermute(value, "seq", [(i, i ^ 1) for i in range(Y * C)])


def to_next_section(value, flip):
    size = Z * X
    return lax.ppermute(value, ("section", "tp"), [(i, size + (i ^ flip)) for i in range(size)])


def gathered_seq(value):
    far = {(0, 0): value, (0, 1): across_core(value)}
    for step in RING:
        far[step, 0] = along_y(value, step)
    for step in RING:
        far[step, 1] = across_core(far[step, 0])
    return [far[piece] for piece in PIECES]


def spread_z(pair):
    received = {step: along_z(pair, step) for step in RING}
    return [pair] + [received[step] for step in (1, 2, 3)]


def normed(rows, shift, scale):
    mean_value = jnp.mean(rows, axis=-1, keepdims=True)
    centred = rows - mean_value
    variance = jnp.mean(centred * centred, axis=-1, keepdims=True)
    return centred * lax.rsqrt(variance + EPSILON) * (1.0 + scale) + shift


def mm(left, right):
    return jnp.dot(left, right, preferred_element_type=F32)


def mm_t(left, right):
    return lax.dot_general(left, right, (((1,), (1,)), ((), ())), preferred_element_type=F32)


def project_all(image_rows, text_rows, w_image, w_text, q_image, q_text, kv, kv_text):
    width = q_image.shape[1]
    image = image_rows[...]
    text = text_rows[...].astype(BF16)
    q_image[...] = mm_t(image, w_image[0:width, :]).astype(BF16)
    q_text[...] = mm_t(text, w_text[0:width, :]).astype(BF16).astype(F32)
    keys_values = mm_t(w_image[width:, :], image).astype(BF16)
    text_kv = mm_t(text, w_text[width:, :]).astype(BF16)
    kv_text[...] = text_kv
    span, count = SLOTS * PT, SLOTS * TQ
    for r in range(REQ):
        kv[r, 0 : 2 * width, :] = keys_values[:, r * span : (r + 1) * span]
        for i in range(2 * width // LANES):
            at = 2 * width + i * count
            kv[r, at : at + count, :] = text_kv[
                r * count : (r + 1) * count, i * LANES : (i + 1) * LANES
            ]


def project_first(place, image, text, mod_image, mod_text, *refs):
    weights, outs, own, (image_rows, text_rows) = refs[:2], refs[2:6], refs[6], refs[7:]
    tp = place[2]
    own[0:PT, :] = image[tp]
    own[PT:ROWS, :] = text[tp]
    for r in range(REQ):
        span, count = SLOTS * PT, SLOTS * TQ
        rows = image[r * SLOTS : (r + 1) * SLOTS].astype(F32).reshape(span, image.shape[2])
        image_rows[r * span : (r + 1) * span, :] = normed(
            rows, mod_image[0, r : r + 1], mod_image[1, r : r + 1]
        ).astype(BF16)
        rows = text[r * SLOTS : (r + 1) * SLOTS].astype(F32).reshape(count, text.shape[2])
        text_rows[r * count : (r + 1) * count, :] = normed(
            rows, mod_text[0, r : r + 1], mod_text[1, r : r + 1]
        )
    project_all(image_rows, text_rows, *weights, *outs)


def chunk_at(place, step, flip):
    return (place[0] + Z - step) % Z * X + (place[1] + flip) % X


def project_next(place, p0, p1, p2, p3, mod_image, mod_text, *refs):
    weights, outs, (image_rows, text_rows) = refs[:2], refs[2:6], refs[6:]
    for step, piece in enumerate((p0, p1, p2, p3)):
        for flip in range(X):
            chunk = chunk_at(place, step, flip)
            r = chunk // SLOTS
            image_rows[pl.ds(pl.multiple_of(chunk * PT, PT), PT), :] = normed(
                piece[flip, 0:PT, :].astype(F32),
                mod_image[0, pl.ds(r, 1), :],
                mod_image[1, pl.ds(r, 1), :],
            ).astype(BF16)
            text_rows[pl.ds(pl.multiple_of(chunk * TQ, TQ), TQ), :] = normed(
                piece[flip, PT:ROWS, :].astype(F32),
                mod_text[0, pl.ds(r, 1), :],
                mod_text[1, pl.ds(r, 1), :],
            )
    project_all(image_rows, text_rows, *weights, *outs)


def slot_of(patch, order):
    return sum(jnp.where(patch == order[k], k, 0) for k in range(SLOTS))


def attend(order, bias, q_image, q_text, *refs):
    fresh, stale = refs[0:8], refs[8:16]
    out_image, out_text, out, o_image, o_text = refs[16:]
    width = q_image.shape[1]
    heads = width // HD
    span, count = SLOTS * PT, SLOTS * TQ
    rows = span + count
    image_keys = len(fresh) * span
    key_count = image_keys + len(fresh) * count
    head_of_row = lax.broadcasted_iota(jnp.int32, (rows, width), 1) // HD
    row = lax.broadcasted_iota(jnp.int32, (rows, 1), 0)
    row_slot = jnp.where(row < span, slot_of(row // PT, order), (row - span) // TQ)
    key = lax.broadcasted_iota(jnp.int32, (1, key_count), 1)
    key_slot = jnp.where(
        key < image_keys, slot_of(key % span // PT, order), (key - image_keys) % count // TQ
    )
    is_fresh = key_slot <= row_slot

    def text_of(pieces, r):
        return jnp.concatenate(
            [
                jnp.concatenate(
                    [
                        piece[r, 2 * width + i * count : 2 * width + (i + 1) * count, :]
                        for i in range(2 * width // LANES)
                    ],
                    axis=1,
                )
                for piece in pieces
            ],
            axis=0,
        )

    def scores_of(queries, pieces, text, r):
        keys = jnp.concatenate([piece[r, 0:width, :] for piece in pieces], axis=1)
        return jnp.concatenate([mm(queries, keys), mm_t(queries, text[:, 0:width])], axis=1)

    def summed_of(weights, pieces, text, r):
        values = jnp.concatenate([piece[r, width : 2 * width, :] for piece in pieces], axis=1)
        return mm_t(weights[:, 0:image_keys], values) + mm(
            weights[:, image_keys:], text[:, width:]
        )

    for r in range(REQ):
        q = jnp.concatenate(
            [
                q_image[r * span : (r + 1) * span, :].astype(F32),
                q_text[r * count : (r + 1) * count, :],
            ],
            axis=0,
        )
        fresh_text, stale_text = text_of(fresh, r), text_of(stale, r)
        merged = jnp.zeros((rows, width), F32)
        for h in range(heads):
            queries = jnp.where(head_of_row == h, q, 0.0).astype(BF16)
            scores = jnp.where(
                is_fresh,
                scores_of(queries, fresh, fresh_text, r),
                scores_of(queries, stale, stale_text, r),
            ) * HD ** (-0.5)
            scores = scores + bias[r : r + 1, :]
            top = jnp.max(scores, axis=-1, keepdims=True)
            weights = jnp.exp(scores - top)
            total = jnp.sum(weights, axis=-1, keepdims=True)
            summed = summed_of(
                jnp.where(is_fresh, weights, 0.0).astype(BF16), fresh, fresh_text, r
            ) + summed_of(jnp.where(is_fresh, 0.0, weights).astype(BF16), stale, stale_text, r)
            merged = jnp.where(head_of_row == h, summed / total, merged)
        o_image[r * span : (r + 1) * span, :] = merged[0:span].astype(BF16)
        o_text[r * count : (r + 1) * count, :] = merged[span:].astype(BF16)
    d_model = out.shape[2]
    image = mm(o_image[...], out_image[...])
    text = mm(o_text[...], out_text[...])
    out[:, 0:PT, :] = image.reshape(CHUNKS, PT, d_model).astype(BF16)
    out[:, PT:ROWS, :] = text.reshape(CHUNKS, TQ, d_model).astype(BF16)


def pack_stale(image, text, out):
    width = image.shape[1]
    count = SLOTS * TQ
    for r in range(REQ):
        out[r, 0:width, :] = image[r]
        for i in range(width // LANES):
            out[r, width + i * count : width + (i + 1) * count, :] = text[
                r, :, i * LANES : (i + 1) * LANES
            ]


def own_mod(mod, i, place):
    return mod[i, pl.ds(place[2] // SLOTS, 1), :]


def summed_chunks(received):
    total = received[0].astype(F32)
    for i in range(1, CHUNKS):
        total = total + received[i].astype(F32)
    return total


def after_attention(place, rows, received, mod_image, mod_text, h1, b):
    summed = summed_chunks(received)
    for low, high, mod in ((0, PT, mod_image), (PT, ROWS, mod_text)):
        first = rows[low:high, :].astype(F32) + own_mod(mod, 2, place) * summed[low:high]
        h1[low:high, :] = first
        b[low:high, :] = normed(
            first, own_mod(mod, 3, place), own_mod(mod, 4, place)
        ).astype(BF16)


def feed_forward(place, p0, p1, p2, p3, up_image, down_image, up_text, down_text, *refs):
    out, image_rows, text_rows = refs
    d_model = out.shape[2]
    for d, piece in enumerate((p0, p1, p2, p3)):
        for flip in range(X):
            at = d * X + flip
            image_rows[at * PT : (at + 1) * PT, :] = piece[flip, 0:PT, :]
            text_rows[at * TQ : (at + 1) * TQ, :] = piece[flip, PT:ROWS, :].astype(F32)
    hidden = jax.nn.gelu(mm(image_rows[...], up_image[...]), approximate=True).astype(BF16)
    image = mm(hidden, down_image[...])
    hidden = jax.nn.gelu(
        mm(text_rows[...].astype(BF16), up_text[...]), approximate=True
    ).astype(BF16)
    text = mm(hidden, down_text[...])
    for d in range(Z):
        for flip in range(X):
            at = d * X + flip
            chunk = chunk_at(place, d, flip)
            out[chunk, 0:PT, :] = image[at * PT : (at + 1) * PT].astype(BF16)
            out[chunk, PT:ROWS, :] = text[at * TQ : (at + 1) * TQ].astype(BF16)


def layer_rows(place, h1, received, mod_image, mod_text):
    summed = summed_chunks(received)
    image = (h1[0:PT, :] + own_mod(mod_image, 5, place) * summed[0:PT]).astype(BF16)
    text = (h1[PT:ROWS, :] + own_mod(mod_text, 5, place) * summed[PT:ROWS]).astype(BF16)
    return image, text


def after_mlp(place, h1, received, mod_image, mod_text, y):
    image, text = layer_rows(place, h1, received, mod_image, mod_text)
    y[0:PT, :] = image
    y[PT:ROWS, :] = text


def last_rows(place, h1, received, mod_image, mod_text, mod_final, weight, first, out):
    image, text = layer_rows(place, h1, received, mod_image, mod_text)
    r = place[2] // SLOTS
    rows = normed(
        image.astype(F32), mod_final[pl.ds(r, 1), 0, :], mod_final[pl.ds(r, 1), 1, :]
    ).astype(BF16)
    velocity = mm_t(weight[...], rows)
    width = text.shape[-1]
    text = jnp.where(place[3] == 0, first[PT:ROWS, :].astype(F32), text.astype(F32))
    out[:, 0:width] = text.astype(BF16)
    out[:, width:] = jnp.concatenate(
        [velocity[i * TQ : (i + 1) * TQ] for i in range(velocity.shape[0] // TQ)], axis=1
    ).astype(BF16)


def outputs(place, factor, received, latent, latent_out, text_out):
    width = text_out.shape[-1]
    count = place[3] * CHUNKS
    for chunk in range(CHUNKS):
        text_out[chunk] = received[count + chunk, :, 0:width]
    for r in range(REQ):
        rows = [
            received[CHUNKS + r * SLOTS + p, :, width:].astype(F32) for p in range(SLOTS)
        ]
        for i in range(latent.shape[1] // TQ):
            velocity = jnp.concatenate([each[:, i * PT : (i + 1) * PT] for each in rows], axis=1)
            at = slice(i * TQ, (i + 1) * TQ)
            latent_out[r, at, :] = latent[r, at, :] + factor[r] * velocity


def sigma_of(index_value):
    progress = 1.0 - index_value / STEPS
    return TIME_SHIFT * progress / (1.0 + (TIME_SHIFT - 1.0) * progress)


def on_device(
    hidden_image,
    hidden_text,
    latent,
    timestep,
    text_length,
    text_keep,
    patch_order,
    stale_image_kv,
    stale_text_kv,
    mod_image,
    mod_text,
    mod_final,
    qkv_image,
    out_image,
    up_image,
    down_image,
    qkv_text,
    out_text,
    up_text,
    down_text,
    final_weight,
):
    d_model = hidden_image.shape[2]
    width = qkv_image.shape[3]
    channels = latent.shape[2]
    section = lax.axis_index("section")
    tp = lax.axis_index("tp")
    seq = lax.axis_index("seq")
    place = jnp.stack([tp // X, tp % X, tp, section]).astype(jnp.int32)
    span, count = SLOTS * PT, SLOTS * TQ
    packed_rows = 2 * width + count * 2 * width // LANES
    packed = ((REQ, packed_rows, LANES), BF16)

    stale_image = jnp.transpose(stale_image_kv[0], (0, 2, 3, 1)).reshape(REQ, 2 * width, span)
    stale_text = stale_text_kv[0].reshape(REQ, count, 2 * width)
    (stale,) = call(pack_stale, "pack_stale", [VMEM] * 2, [packed])(stale_image, stale_text)
    stale_pieces = gathered_seq(stale)

    positions = jnp.arange(text_keep.shape[1], dtype=jnp.int32)
    valid = (positions[None, :] < text_length[:, None]) & (text_keep == 1)
    text_bias = jnp.where(valid, 0.0, NEGATIVE).astype(F32).reshape(REQ, Y * C, count)
    piece_seq = [(seq // C + Y - step) % Y * C + (seq + flip) % C for step, flip in PIECES]
    text_bias = jnp.concatenate(
        [lax.dynamic_index_in_dim(text_bias, each, 1, keepdims=False) for each in piece_seq], axis=1
    )
    bias = jnp.concatenate([jnp.zeros((REQ, Y * C * span), F32), text_bias], axis=1)

    def flat_qkv(weight):
        return jnp.transpose(weight[0], (1, 2, 0)).reshape(3 * width, d_model)

    weights = flat_qkv(qkv_image), flat_qkv(qkv_text)
    mods = jnp.transpose(mod_image[0], (1, 0, 2)), jnp.transpose(mod_text[0], (1, 0, 2))

    qkv_shapes = [
        ((CHUNKS * PT, width), BF16),
        ((CHUNKS * TQ, width), F32),
        packed,
        ((CHUNKS * TQ, 2 * width), BF16),
    ]
    rows_scratch = [
        pltpu.VMEM((CHUNKS * PT, d_model), BF16),
        pltpu.VMEM((CHUNKS * TQ, d_model), F32),
    ]
    chunks = ((CHUNKS, ROWS, d_model), BF16)
    row_f32, row_bf16 = ((ROWS, d_model), F32), ((ROWS, d_model), BF16)

    def exchanged(value):
        return lax.all_to_all(value, "tp", 0, 0, tiled=True)

    def rest_of_layer(q_image, q_text, kv, rows):
        (partial,) = call(
            attend,
            "attend",
            [SMEM] + [VMEM] * 21,
            [chunks],
            [pltpu.VMEM((CHUNKS * PT, width), BF16), pltpu.VMEM((CHUNKS * TQ, width), BF16)],
        )(
            patch_order,
            bias,
            q_image,
            q_text,
            *gathered_seq(kv),
            *stale_pieces,
            out_image[0],
            out_text[0],
        )
        h1, b = call(
            after_attention, "after_attention", [SMEM] + [VMEM] * 4, [row_f32, row_bf16]
        )(place, rows, exchanged(partial), *mods)
        pieces = spread_z(jnp.stack([b, across_x(b)]))
        (partial,) = call(
            feed_forward, "feed_forward", [SMEM] + [VMEM] * 8, [chunks], rows_scratch
        )(place, *pieces, up_image[0], down_image[0], up_text[0], down_text[0])
        return h1, exchanged(partial)

    q_image, q_text, kv_first, kv_text_first, own_rows = call(
        project_first, "project_first", [SMEM] + [VMEM] * 6, qkv_shapes + [row_bf16], rows_scratch
    )(
        place,
        hidden_image.reshape(CHUNKS, PT, d_model),
        hidden_text.reshape(CHUNKS, TQ, d_model),
        *mods,
        *weights,
    )
    h1, received = rest_of_layer(q_image, q_text, kv_first, own_rows)
    (y_first,) = call(after_mlp, "after_mlp", [SMEM] + [VMEM] * 4, [row_bf16])(
        place, h1, received, *mods
    )
    arrived = to_next_section(y_first, 0)
    pieces = spread_z(jnp.stack([arrived, to_next_section(y_first, 1)]))
    q_image, q_text, kv_next, kv_text_next = call(
        project_next, "project_next", [SMEM] + [VMEM] * 8, qkv_shapes, rows_scratch
    )(place, *pieces, *mods, *weights)
    h1, received = rest_of_layer(q_image, q_text, kv_next, arrived)
    tail = ((TQ, d_model + PT * channels // TQ), BF16)
    (tail_rows,) = call(last_rows, "last_rows", [SMEM] + [VMEM] * 7, [tail])(
        place, h1, received, *mods, mod_final, jnp.transpose(final_weight), y_first
    )
    shared = lax.all_to_all(
        jnp.broadcast_to(tail_rows[None], (2 * CHUNKS,) + tail_rows.shape),
        ("section", "tp"),
        0,
        0,
        tiled=True,
    )
    index_value = timestep.astype(F32)
    sigma_now = sigma_of(index_value)
    sigma_next = sigma_of(index_value + 1.0)
    factor = jnp.where(section == 0, sigma_next - sigma_now, -sigma_now)
    latent_part, text_hidden = call(
        outputs,
        "outputs",
        [SMEM] * 2 + [VMEM] * 2,
        [((REQ, channels, span), F32), ((CHUNKS, TQ, d_model), BF16)],
    )(place, factor, shared, jnp.transpose(latent, (0, 2, 1)))
    image_kv = jnp.where(section == 0, kv_first[:, : 2 * width], kv_next[:, : 2 * width])
    text_kv = jnp.where(section == 0, kv_text_first, kv_text_next)
    return (
        jnp.transpose(latent_part, (0, 2, 1))[None],
        jnp.transpose(image_kv.reshape(REQ, 2, width, span), (0, 3, 1, 2))[None],
        text_kv.reshape(1, REQ, count, 2, width),
        text_hidden.reshape(1, REQ, count, d_model),
    )


def solution(mesh):
    in_specs = (
        P(None, "seq", None),
        P(None, "seq", None),
        P(None, "seq", None),
        P(),
        P(),
        P(),
        P(),
        P("section", None, "seq", None, "tp"),
        P("section", None, "seq", None, "tp"),
        P("section", None, None, None),
        P("section", None, None, None),
        P(),
        P("section", None, None, "tp"),
        P("section", "tp", None),
        P("section", None, "tp"),
        P("section", "tp", None),
        P("section", None, None, "tp"),
        P("section", "tp", None),
        P("section", None, "tp"),
        P("section", "tp", None),
        P(),
    )
    out_specs = (
        P("section", None, "seq", None),
        P("section", None, "seq", None, "tp"),
        P("section", None, "seq", None, "tp"),
        P("section", None, "seq", None),
    )
    return jax.shard_map(
        on_device, mesh=mesh, in_specs=in_specs, out_specs=out_specs, check_vma=False
    )
```

```python
import jax
import jax.numpy as jnp
from jax import lax
from jax.experimental import pallas as pl
from jax.experimental.pallas import tpu as pltpu
from jax.sharding import PartitionSpec as P

HD = 64
STEPS = 28
EPSILON = 1e-06
NEGATIVE = -1e30
TIME_SHIFT = 3.0

F32 = jnp.float32
BF16 = jnp.bfloat16

REQ, SLOTS, PT, TQ = 2, 4, 32, 8
ROWS = PT + TQ
CHUNKS = REQ * SLOTS
Z, X = 4, 2
Y, C = 4, 2
LANES = 128
RING = (1, 3, 2)
PIECES = ((0, 0), (0, 1), (1, 0), (1, 1), (3, 0), (3, 1), (2, 0), (2, 1))

VMEM = pl.BlockSpec(memory_space=pltpu.VMEM)
SMEM = pl.BlockSpec(memory_space=pltpu.SMEM)


def call(body, name, in_specs, out_shapes, scratch=()):
    return pl.pallas_call(
        body,
        name=name,
        in_specs=list(in_specs),
        out_specs=[VMEM] * len(out_shapes),
        out_shape=[jax.ShapeDtypeStruct(*each) for each in out_shapes],
        scratch_shapes=list(scratch),
        compiler_params=pltpu.CompilerParams(vmem_limit_bytes=40 * 1024 * 1024),
    )


def along_z(value, step):
    pairs = [(z * X + x, (z + step) % Z * X + x) for z in range(Z) for x in range(X)]
    return lax.ppermute(value, "tp", pairs)


def across_x(value):
    return lax.ppermute(value, "tp", [(i, i ^ 1) for i in range(Z * X)])


def along_y(value, step):
    pairs = [(y * C + c, (y + step) % Y * C + c) for y in range(Y) for c in range(C)]
    return lax.ppermute(value, "seq", pairs)


def across_core(value):
    return lax.ppermute(value, "seq", [(i, i ^ 1) for i in range(Y * C)])


def to_next_section(value, flip):
    size = Z * X
    return lax.ppermute(value, ("section", "tp"), [(i, size + (i ^ flip)) for i in range(size)])


def gathered_seq(value):
    far = {(0, 0): value, (0, 1): across_core(value)}
    for step in RING:
        far[step, 0] = along_y(value, step)
    for step in RING:
        far[step, 1] = across_core(far[step, 0])
    return [far[piece] for piece in PIECES]


def spread_z(pair):
    received = {step: along_z(pair, step) for step in RING}
    return [pair] + [received[step] for step in (1, 2, 3)]


def normed(rows, shift, scale):
    mean_value = jnp.mean(rows, axis=-1, keepdims=True)
    centred = rows - mean_value
    variance = jnp.mean(centred * centred, axis=-1, keepdims=True)
    return centred * lax.rsqrt(variance + EPSILON) * (1.0 + scale) + shift


def mm(left, right):
    return jnp.dot(left, right, preferred_element_type=F32)


def mm_t(left, right):
    return lax.dot_general(left, right, (((1,), (1,)), ((), ())), preferred_element_type=F32)


def project_all(image_rows, text_rows, w_image, w_text, q_image, q_text, kv, kv_text):
    width = q_image.shape[1]
    image = image_rows[...]
    text = text_rows[...].astype(BF16)
    q_image[...] = mm_t(image, w_image[0:width, :]).astype(BF16)
    q_text[...] = mm_t(text, w_text[0:width, :]).astype(BF16).astype(F32)
    keys_values = mm_t(w_image[width:, :], image).astype(BF16)
    text_kv = mm_t(text, w_text[width:, :]).astype(BF16)
    kv_text[...] = text_kv
    span, count = SLOTS * PT, SLOTS * TQ
    for r in range(REQ):
        kv[r, 0 : 2 * width, :] = keys_values[:, r * span : (r + 1) * span]
        for i in range(2 * width // LANES):
            at = 2 * width + i * count
            kv[r, at : at + count, :] = text_kv[
                r * count : (r + 1) * count, i * LANES : (i + 1) * LANES
            ]


def project_first(place, image, text, mod_image, mod_text, *refs):
    weights, outs, own, (image_rows, text_rows) = refs[:2], refs[2:6], refs[6], refs[7:]
    tp = place[2]
    own[0:PT, :] = image[tp]
    own[PT:ROWS, :] = text[tp]
    for r in range(REQ):
        span, count = SLOTS * PT, SLOTS * TQ
        rows = image[r * SLOTS : (r + 1) * SLOTS].astype(F32).reshape(span, image.shape[2])
        image_rows[r * span : (r + 1) * span, :] = normed(
            rows, mod_image[0, r : r + 1], mod_image[1, r : r + 1]
        ).astype(BF16)
        rows = text[r * SLOTS : (r + 1) * SLOTS].astype(F32).reshape(count, text.shape[2])
        text_rows[r * count : (r + 1) * count, :] = normed(
            rows, mod_text[0, r : r + 1], mod_text[1, r : r + 1]
        )
    project_all(image_rows, text_rows, *weights, *outs)


def chunk_at(place, step, flip):
    return (place[0] + Z - step) % Z * X + (place[1] + flip) % X


def project_next(place, p0, p1, p2, p3, mod_image, mod_text, *refs):
    weights, outs, (image_rows, text_rows) = refs[:2], refs[2:6], refs[8:]
    image_out, text_out = refs[6:8]
    for step, piece in enumerate((p0, p1, p2, p3)):
        for flip in range(X):
            chunk = chunk_at(place, step, flip)
            r = chunk // SLOTS
            image_out[chunk] = piece[flip, 0:PT, :]
            text_out[chunk] = piece[flip, PT:ROWS, :]
            image_rows[pl.ds(pl.multiple_of(chunk * PT, PT), PT), :] = normed(
                piece[flip, 0:PT, :].astype(F32),
                mod_image[0, pl.ds(r, 1), :],
                mod_image[1, pl.ds(r, 1), :],
            ).astype(BF16)
            text_rows[pl.ds(pl.multiple_of(chunk * TQ, TQ), TQ), :] = normed(
                piece[flip, PT:ROWS, :].astype(F32),
                mod_text[0, pl.ds(r, 1), :],
                mod_text[1, pl.ds(r, 1), :],
            )
    project_all(image_rows, text_rows, *weights, *outs)


def slot_of(patch, order):
    return sum(jnp.where(patch == order[k], k, 0) for k in range(SLOTS))


def attended(order, bias, q_image, q_text, fresh, stale):
    width = q_image.shape[1]
    heads = width // HD
    span, count = SLOTS * PT, SLOTS * TQ
    rows = span + count
    image_keys = len(fresh) * span
    key_count = image_keys + len(fresh) * count
    head_of_row = lax.broadcasted_iota(jnp.int32, (rows, width), 1) // HD
    row = lax.broadcasted_iota(jnp.int32, (rows, 1), 0)
    row_slot = jnp.where(row < span, slot_of(row // PT, order), (row - span) // TQ)
    key = lax.broadcasted_iota(jnp.int32, (1, key_count), 1)
    key_slot = jnp.where(
        key < image_keys, slot_of(key % span // PT, order), (key - image_keys) % count // TQ
    )
    is_fresh = key_slot <= row_slot

    def text_of(pieces, r):
        return jnp.concatenate(
            [
                jnp.concatenate(
                    [
                        piece[r, 2 * width + i * count : 2 * width + (i + 1) * count, :]
                        for i in range(2 * width // LANES)
                    ],
                    axis=1,
                )
                for piece in pieces
            ],
            axis=0,
        )

    def scores_of(queries, pieces, text, r):
        keys = jnp.concatenate([piece[r, 0:width, :] for piece in pieces], axis=1)
        return jnp.concatenate([mm(queries, keys), mm_t(queries, text[:, 0:width])], axis=1)

    def summed_of(weights, pieces, text, r):
        values = jnp.concatenate([piece[r, width : 2 * width, :] for piece in pieces], axis=1)
        return mm_t(weights[:, 0:image_keys], values) + mm(
            weights[:, image_keys:], text[:, width:]
        )

    for r in range(REQ):
        q = jnp.concatenate(
            [
                q_image[r * span : (r + 1) * span, :].astype(F32),
                q_text[r * count : (r + 1) * count, :],
            ],
            axis=0,
        )
        fresh_text, stale_text = text_of(fresh, r), text_of(stale, r)
        merged = jnp.zeros((rows, width), F32)
        for h in range(heads):
            queries = jnp.where(head_of_row == h, q, 0.0).astype(BF16)
            scores = jnp.where(
                is_fresh,
                scores_of(queries, fresh, fresh_text, r),
                scores_of(queries, stale, stale_text, r),
            ) * HD ** (-0.5)
            scores = scores + bias[r : r + 1, :]
            top = jnp.max(scores, axis=-1, keepdims=True)
            weights = jnp.exp(scores - top)
            total = jnp.sum(weights, axis=-1, keepdims=True)
            summed = summed_of(
                jnp.where(is_fresh, weights, 0.0).astype(BF16), fresh, fresh_text, r
            ) + summed_of(jnp.where(is_fresh, 0.0, weights).astype(BF16), stale, stale_text, r)
            merged = jnp.where(head_of_row == h, summed / total, merged)
        yield r, merged[0:span].astype(BF16), merged[span:].astype(BF16)


def attend_project(order, bias, q_image, q_text, *refs):
    fresh, stale = refs[0:8], refs[8:16]
    out_image, out_text, out, o_image, o_text = refs[16:]
    span, count = SLOTS * PT, SLOTS * TQ
    for r, image, text in attended(order, bias, q_image, q_text, fresh, stale):
        o_image[r * span : (r + 1) * span, :] = image
        o_text[r * count : (r + 1) * count, :] = text
    d_model = out.shape[2]
    image = mm(o_image[...], out_image[...])
    text = mm(o_text[...], out_text[...])
    out[:, 0:PT, :] = image.reshape(CHUNKS, PT, d_model).astype(BF16)
    out[:, PT:ROWS, :] = text.reshape(CHUNKS, TQ, d_model).astype(BF16)


def attend_heads(order, bias, q_image, q_text, *refs):
    fresh, stale, out = refs[0:8], refs[8:16], refs[16]
    rows = SLOTS * ROWS
    for r, image, text in attended(order, bias, q_image, q_text, fresh, stale):
        heads = jnp.concatenate([image, text], axis=0)
        out[r * rows : (r + 1) * rows, :] = heads[:, 0:LANES]
        half = heads.shape[1] - LANES
        at = REQ * rows
        out[at : at + rows, r * half : (r + 1) * half] = heads[:, LANES:]


def pack_stale(image, text, out):
    width = image.shape[1]
    count = SLOTS * TQ
    for r in range(REQ):
        out[r, 0:width, :] = image[r]
        for i in range(width // LANES):
            out[r, width + i * count : width + (i + 1) * count, :] = text[
                r, :, i * LANES : (i + 1) * LANES
            ]


def own_mod(mod, i, place):
    return mod[i, pl.ds(place[2] // SLOTS, 1), :]


def summed_chunks(received):
    total = received[0].astype(F32)
    for i in range(1, CHUNKS):
        total = total + received[i].astype(F32)
    return total


def after_attention(place, rows, received, mod_image, mod_text, h1, b):
    summed = summed_chunks(received)
    for low, high, mod in ((0, PT, mod_image), (PT, ROWS, mod_text)):
        first = rows[low:high, :].astype(F32) + own_mod(mod, 2, place) * summed[low:high]
        h1[low:high, :] = first
        b[low:high, :] = normed(
            first, own_mod(mod, 3, place), own_mod(mod, 4, place)
        ).astype(BF16)


def feed_forward(place, p0, p1, p2, p3, up_image, down_image, up_text, down_text, *refs):
    out, image_rows, text_rows = refs
    d_model = out.shape[2]
    for d, piece in enumerate((p0, p1, p2, p3)):
        for flip in range(X):
            at = d * X + flip
            image_rows[at * PT : (at + 1) * PT, :] = piece[flip, 0:PT, :]
            text_rows[at * TQ : (at + 1) * TQ, :] = piece[flip, PT:ROWS, :].astype(F32)
    hidden = jax.nn.gelu(mm(image_rows[...], up_image[...]), approximate=True).astype(BF16)
    image = mm(hidden, down_image[...])
    hidden = jax.nn.gelu(
        mm(text_rows[...].astype(BF16), up_text[...]), approximate=True
    ).astype(BF16)
    text = mm(hidden, down_text[...])
    for d in range(Z):
        for flip in range(X):
            at = d * X + flip
            chunk = chunk_at(place, d, flip)
            out[chunk, 0:PT, :] = image[at * PT : (at + 1) * PT].astype(BF16)
            out[chunk, PT:ROWS, :] = text[at * TQ : (at + 1) * TQ].astype(BF16)


def heads_mlp(place, o0, o1, o2, o3, image, text, w_own, w_other, *refs):
    up_image, down_image, up_text, down_text, mod_image, mod_text = refs[:6]
    out, own, o_image, o_text, image_h1, text_h1, image_rows, text_rows = refs[6:]
    d_model = out.shape[2]
    span, count, rows = SLOTS * PT, SLOTS * TQ, SLOTS * ROWS
    for step, piece in enumerate((o0, o1, o2, o3)):
        from_z = (place[0] + Z - step) % Z
        low, high = place[1], 1 - place[1]
        for r in range(REQ):
            half = LANES // REQ
            parts = []
            for source in (low, high):
                parts.append(piece[source, r * rows : (r + 1) * rows, :])
                parts.append(
                    piece[source, REQ * rows : REQ * rows + rows, r * half : (r + 1) * half]
                )
            heads = jnp.concatenate(parts, axis=1)
            lanes = pl.ds(pl.multiple_of(from_z * heads.shape[1], LANES), heads.shape[1])
            o_image[r * span : (r + 1) * span, lanes] = heads[0:span]
            o_text[r * count : (r + 1) * count, lanes] = heads[span:]

    def projected(w_image, w_text):
        image_h1[...] = mm(o_image[...], w_image[...])
        text_h1[...] = mm(o_text[...], w_text[...])

    @pl.when(place[4] == 0)
    def _():
        projected(w_own, w_other)

    @pl.when(place[4] != 0)
    def _():
        projected(w_other, w_own)

    for rows_in, h1, b, mod, size in (
        (image, image_h1, image_rows, mod_image, PT),
        (text, text_h1, text_rows, mod_text, TQ),
    ):
        for r in range(REQ):
            at = slice(r * SLOTS * size, (r + 1) * SLOTS * size)
            x = rows_in[r * SLOTS : (r + 1) * SLOTS].astype(F32).reshape(SLOTS * size, d_model)
            first = x + mod[2, r : r + 1] * h1[at, :]
            h1[at, :] = first
            b[at, :] = normed(first, mod[3, r : r + 1], mod[4, r : r + 1]).astype(BF16)
    tp = place[2]
    own[0:PT, :] = image_h1[pl.ds(pl.multiple_of(tp * PT, PT), PT), :]
    own[PT:ROWS, :] = text_h1[pl.ds(pl.multiple_of(tp * TQ, TQ), TQ), :]
    hidden = jax.nn.gelu(mm(image_rows[...], up_image[...]), approximate=True).astype(BF16)
    out[:, 0:PT, :] = mm(hidden, down_image[...]).reshape(CHUNKS, PT, d_model).astype(BF16)
    hidden = jax.nn.gelu(mm(text_rows[...], up_text[...]), approximate=True).astype(BF16)
    out[:, PT:ROWS, :] = mm(hidden, down_text[...]).reshape(CHUNKS, TQ, d_model).astype(BF16)


def layer_rows(place, h1, received, mod_image, mod_text):
    summed = summed_chunks(received)
    image = (h1[0:PT, :] + own_mod(mod_image, 5, place) * summed[0:PT]).astype(BF16)
    text = (h1[PT:ROWS, :] + own_mod(mod_text, 5, place) * summed[PT:ROWS]).astype(BF16)
    return image, text


def after_mlp(place, h1, received, mod_image, mod_text, y):
    image, text = layer_rows(place, h1, received, mod_image, mod_text)
    y[0:PT, :] = image
    y[PT:ROWS, :] = text


def last_rows(place, h1, received, mod_image, mod_text, mod_final, weight, first, out):
    image, text = layer_rows(place, h1, received, mod_image, mod_text)
    r = place[2] // SLOTS
    rows = normed(
        image.astype(F32), mod_final[pl.ds(r, 1), 0, :], mod_final[pl.ds(r, 1), 1, :]
    ).astype(BF16)
    velocity = mm_t(weight[...], rows)
    width = text.shape[-1]
    text = jnp.where(place[3] == 0, first[PT:ROWS, :].astype(F32), text.astype(F32))
    out[:, 0:width] = text.astype(BF16)
    out[:, width:] = jnp.concatenate(
        [velocity[i * TQ : (i + 1) * TQ] for i in range(velocity.shape[0] // TQ)], axis=1
    ).astype(BF16)


def outputs(place, factor, received, latent, latent_out, text_out):
    width = text_out.shape[-1]
    count = place[3] * CHUNKS
    for chunk in range(CHUNKS):
        text_out[chunk] = received[count + chunk, :, 0:width]
    for r in range(REQ):
        rows = [
            received[CHUNKS + r * SLOTS + p, :, width:].astype(F32) for p in range(SLOTS)
        ]
        for i in range(latent.shape[1] // TQ):
            velocity = jnp.concatenate([each[:, i * PT : (i + 1) * PT] for each in rows], axis=1)
            at = slice(i * TQ, (i + 1) * TQ)
            latent_out[r, at, :] = latent[r, at, :] + factor[r] * velocity


def sigma_of(index_value):
    progress = 1.0 - index_value / STEPS
    return TIME_SHIFT * progress / (1.0 + (TIME_SHIFT - 1.0) * progress)


def on_device(
    hidden_image,
    hidden_text,
    latent,
    timestep,
    text_length,
    text_keep,
    patch_order,
    stale_image_kv,
    stale_text_kv,
    mod_image,
    mod_text,
    mod_final,
    qkv_image,
    out_image,
    up_image,
    down_image,
    qkv_text,
    out_text,
    up_text,
    down_text,
    final_weight,
):
    d_model = hidden_image.shape[2]
    width = qkv_image.shape[3]
    channels = latent.shape[2]
    section = lax.axis_index("section")
    tp = lax.axis_index("tp")
    seq = lax.axis_index("seq")
    place = jnp.stack([tp // X, tp % X, tp, section, seq % C]).astype(jnp.int32)
    span, count = SLOTS * PT, SLOTS * TQ
    packed_rows = 2 * width + count * 2 * width // LANES
    packed = ((REQ, packed_rows, LANES), BF16)

    stale_image = jnp.transpose(stale_image_kv[0], (0, 2, 3, 1)).reshape(REQ, 2 * width, span)
    stale_text = stale_text_kv[0].reshape(REQ, count, 2 * width)
    (stale,) = call(pack_stale, "pack_stale", [VMEM] * 2, [packed])(stale_image, stale_text)
    stale_pieces = gathered_seq(stale)

    positions = jnp.arange(text_keep.shape[1], dtype=jnp.int32)
    valid = (positions[None, :] < text_length[:, None]) & (text_keep == 1)
    text_bias = jnp.where(valid, 0.0, NEGATIVE).astype(F32).reshape(REQ, Y * C, count)
    piece_seq = [(seq // C + Y - step) % Y * C + (seq + flip) % C for step, flip in PIECES]
    text_bias = jnp.concatenate(
        [lax.dynamic_index_in_dim(text_bias, each, 1, keepdims=False) for each in piece_seq], axis=1
    )
    bias = jnp.concatenate([jnp.zeros((REQ, Y * C * span), F32), text_bias], axis=1)

    def flat_qkv(weight):
        return jnp.transpose(weight[0], (1, 2, 0)).reshape(3 * width, d_model)

    weights = flat_qkv(qkv_image), flat_qkv(qkv_text)
    mods = jnp.transpose(mod_image[0], (1, 0, 2)), jnp.transpose(mod_text[0], (1, 0, 2))

    qkv_shapes = [
        ((CHUNKS * PT, width), BF16),
        ((CHUNKS * TQ, width), F32),
        packed,
        ((CHUNKS * TQ, 2 * width), BF16),
    ]
    rows_scratch = [
        pltpu.VMEM((CHUNKS * PT, d_model), BF16),
        pltpu.VMEM((CHUNKS * TQ, d_model), F32),
    ]
    chunks = ((CHUNKS, ROWS, d_model), BF16)
    row_f32, row_bf16 = ((ROWS, d_model), F32), ((ROWS, d_model), BF16)

    def exchanged(value):
        return lax.all_to_all(value, "tp", 0, 0, tiled=True)

    w_own = lax.all_gather(
        jnp.where(seq % C == 0, out_image[0], out_text[0]), "tp", axis=0, tiled=True
    )
    w_other = across_core(w_own)
    mlp = up_image[0], down_image[0], up_text[0], down_text[0]

    def rest_by_sums(q_image, q_text, kv, rows):
        (partial,) = call(
            attend_project,
            "attend_project",
            [SMEM] + [VMEM] * 21,
            [chunks],
            [pltpu.VMEM((CHUNKS * PT, width), BF16), pltpu.VMEM((CHUNKS * TQ, width), BF16)],
        )(
            patch_order,
            bias,
            q_image,
            q_text,
            *gathered_seq(kv),
            *stale_pieces,
            out_image[0],
            out_text[0],
        )
        h1, b = call(
            after_attention, "after_attention", [SMEM] + [VMEM] * 4, [row_f32, row_bf16]
        )(place, rows, exchanged(partial), *mods)
        pieces = spread_z(jnp.stack([b, across_x(b)]))
        (partial,) = call(
            feed_forward, "feed_forward", [SMEM] + [VMEM] * 8, [chunks], rows_scratch
        )(place, *pieces, *mlp)
        return h1, exchanged(partial)

    def rest_by_heads(q_image, q_text, kv, image_all, text_all):
        heads = ((REQ * SLOTS * ROWS * width // LANES, LANES), BF16)
        (o,) = call(attend_heads, "attend_heads", [SMEM] + [VMEM] * 19, [heads])(
            patch_order, bias, q_image, q_text, *gathered_seq(kv), *stale_pieces
        )
        pieces = spread_z(jnp.stack([o, across_x(o)]))
        partial, h1 = call(
            heads_mlp,
            "heads_mlp",
            [SMEM] + [VMEM] * 14,
            [chunks, row_f32],
            [
                pltpu.VMEM((CHUNKS * PT, d_model), BF16),
                pltpu.VMEM((CHUNKS * TQ, d_model), BF16),
                pltpu.VMEM((CHUNKS * PT, d_model), F32),
                pltpu.VMEM((CHUNKS * TQ, d_model), F32),
                pltpu.VMEM((CHUNKS * PT, d_model), BF16),
                pltpu.VMEM((CHUNKS * TQ, d_model), BF16),
            ],
        )(place, *pieces, image_all, text_all, w_own, w_other, *mlp, *mods)
        return h1, exchanged(partial)

    q_image, q_text, kv_first, kv_text_first, own_rows = call(
        project_first, "project_first", [SMEM] + [VMEM] * 6, qkv_shapes + [row_bf16], rows_scratch
    )(
        place,
        hidden_image.reshape(CHUNKS, PT, d_model),
        hidden_text.reshape(CHUNKS, TQ, d_model),
        *mods,
        *weights,
    )
    h1, received = rest_by_sums(q_image, q_text, kv_first, own_rows)
    (y_first,) = call(after_mlp, "after_mlp", [SMEM] + [VMEM] * 4, [row_bf16])(
        place, h1, received, *mods
    )
    arrived = to_next_section(y_first, 0)
    pieces = spread_z(jnp.stack([arrived, to_next_section(y_first, 1)]))
    q_image, q_text, kv_next, kv_text_next, image_all, text_all = call(
        project_next,
        "project_next",
        [SMEM] + [VMEM] * 8,
        qkv_shapes + [((CHUNKS, PT, d_model), BF16), ((CHUNKS, TQ, d_model), BF16)],
        rows_scratch,
    )(place, *pieces, *mods, *weights)
    h1, received = rest_by_heads(q_image, q_text, kv_next, image_all, text_all)
    tail = ((TQ, d_model + PT * channels // TQ), BF16)
    (tail_rows,) = call(last_rows, "last_rows", [SMEM] + [VMEM] * 7, [tail])(
        place, h1, received, *mods, mod_final, jnp.transpose(final_weight), y_first
    )
    shared = lax.all_to_all(
        jnp.broadcast_to(tail_rows[None], (2 * CHUNKS,) + tail_rows.shape),
        ("section", "tp"),
        0,
        0,
        tiled=True,
    )
    index_value = timestep.astype(F32)
    sigma_now = sigma_of(index_value)
    sigma_next = sigma_of(index_value + 1.0)
    factor = jnp.where(section == 0, sigma_next - sigma_now, -sigma_now)
    latent_part, text_hidden = call(
        outputs,
        "outputs",
        [SMEM] * 2 + [VMEM] * 2,
        [((REQ, channels, span), F32), ((CHUNKS, TQ, d_model), BF16)],
    )(place, factor, shared, jnp.transpose(latent, (0, 2, 1)))
    image_kv = jnp.where(section == 0, kv_first[:, : 2 * width], kv_next[:, : 2 * width])
    text_kv = jnp.where(section == 0, kv_text_first, kv_text_next)
    return (
        jnp.transpose(latent_part, (0, 2, 1))[None],
        jnp.transpose(image_kv.reshape(REQ, 2, width, span), (0, 3, 1, 2))[None],
        text_kv.reshape(1, REQ, count, 2, width),
        text_hidden.reshape(1, REQ, count, d_model),
    )


def solution(mesh):
    in_specs = (
        P(None, "seq", None),
        P(None, "seq", None),
        P(None, "seq", None),
        P(),
        P(),
        P(),
        P(),
        P("section", None, "seq", None, "tp"),
        P("section", None, "seq", None, "tp"),
        P("section", None, None, None),
        P("section", None, None, None),
        P(),
        P("section", None, None, "tp"),
        P("section", "tp", None),
        P("section", None, "tp"),
        P("section", "tp", None),
        P("section", None, None, "tp"),
        P("section", "tp", None),
        P("section", None, "tp"),
        P("section", "tp", None),
        P(),
    )
    out_specs = (
        P("section", None, "seq", None),
        P("section", None, "seq", None, "tp"),
        P("section", None, "seq", None, "tp"),
        P("section", None, "seq", None),
    )
    return jax.shard_map(
        on_device, mesh=mesh, in_specs=in_specs, out_specs=out_specs, check_vma=False
    )
```

```python
import jax
import jax.numpy as jnp
from jax import lax
from jax.experimental import pallas as pl
from jax.experimental.pallas import tpu as pltpu
from jax.sharding import PartitionSpec as P

HD = 64
STEPS = 28
EPSILON = 1e-06
NEGATIVE = -1e30
TIME_SHIFT = 3.0

F32 = jnp.float32
BF16 = jnp.bfloat16

REQ, SLOTS, PT, TQ = 2, 4, 32, 8
ROWS = PT + TQ
CHUNKS = REQ * SLOTS
Z, X = 4, 2
Y, C = 4, 2
LANES = 128
RING = (2, 1, 3)
PIECES = ((0, 0), (0, 1), (1, 0), (1, 1), (3, 0), (3, 1), (2, 0), (2, 1))

VMEM = pl.BlockSpec(memory_space=pltpu.VMEM)
SMEM = pl.BlockSpec(memory_space=pltpu.SMEM)


def call(body, name, in_specs, out_shapes, scratch=(), mib=40):
    return pl.pallas_call(
        body,
        name=name,
        in_specs=list(in_specs),
        out_specs=[VMEM] * len(out_shapes),
        out_shape=[jax.ShapeDtypeStruct(*each) for each in out_shapes],
        scratch_shapes=list(scratch),
        compiler_params=pltpu.CompilerParams(vmem_limit_bytes=mib * 1024 * 1024),
    )


def along_z(value, step):
    pairs = [(z * X + x, (z + step) % Z * X + x) for z in range(Z) for x in range(X)]
    return lax.ppermute(value, "tp", pairs)


def across_x(value):
    return lax.ppermute(value, "tp", [(i, i ^ 1) for i in range(Z * X)])


def along_y(value, step):
    pairs = [(y * C + c, (y + step) % Y * C + c) for y in range(Y) for c in range(C)]
    return lax.ppermute(value, "seq", pairs)


def across_core(value):
    return lax.ppermute(value, "seq", [(i, i ^ 1) for i in range(Y * C)])


def to_next_section(value, flip):
    size = Z * X
    return lax.ppermute(value, ("section", "tp"), [(i, size + (i ^ flip)) for i in range(size)])


def gathered_seq(value):
    far = {(0, 0): value, (0, 1): across_core(value)}
    for step in RING:
        far[step, 0] = along_y(value, step)
    for step in RING:
        far[step, 1] = across_core(far[step, 0])
    return [far[piece] for piece in PIECES]


def spread_z(pair):
    received = {step: along_z(pair, step) for step in RING}
    return [pair] + [received[step] for step in (1, 2, 3)]


def normed(rows, shift, scale):
    mean_value = jnp.mean(rows, axis=-1, keepdims=True)
    centred = rows - mean_value
    variance = jnp.mean(centred * centred, axis=-1, keepdims=True)
    return centred * lax.rsqrt(variance + EPSILON) * (1.0 + scale) + shift


def mm(left, right):
    return jnp.dot(left, right, preferred_element_type=F32)


def mm_t(left, right):
    return lax.dot_general(left, right, (((1,), (1,)), ((), ())), preferred_element_type=F32)


def project_all(image_rows, text_rows, w_image, w_text, q_image, q_text, kv, kv_text):
    width = q_image.shape[1]
    image = image_rows[...]
    text = text_rows[...].astype(BF16)
    q_image[...] = mm_t(image, w_image[0:width, :]).astype(BF16)
    q_text[...] = mm_t(text, w_text[0:width, :]).astype(BF16).astype(F32)
    keys_values = mm_t(w_image[width:, :], image).astype(BF16)
    text_kv = mm_t(text, w_text[width:, :]).astype(BF16)
    kv_text[...] = text_kv
    span, count = SLOTS * PT, SLOTS * TQ
    for r in range(REQ):
        kv[r, 0 : 2 * width, :] = keys_values[:, r * span : (r + 1) * span]
        for i in range(2 * width // LANES):
            at = 2 * width + i * count
            kv[r, at : at + count, :] = text_kv[
                r * count : (r + 1) * count, i * LANES : (i + 1) * LANES
            ]


def project_first(place, image, text, mod_image, mod_text, *refs):
    weights, outs, own, (image_rows, text_rows) = refs[:2], refs[2:6], refs[6], refs[7:]
    tp = place[2]
    own[0:PT, :] = image[tp]
    own[PT:ROWS, :] = text[tp]
    for r in range(REQ):
        span, count = SLOTS * PT, SLOTS * TQ
        rows = image[r * SLOTS : (r + 1) * SLOTS].astype(F32).reshape(span, image.shape[2])
        image_rows[r * span : (r + 1) * span, :] = normed(
            rows, mod_image[0, r : r + 1], mod_image[1, r : r + 1]
        ).astype(BF16)
        rows = text[r * SLOTS : (r + 1) * SLOTS].astype(F32).reshape(count, text.shape[2])
        text_rows[r * count : (r + 1) * count, :] = normed(
            rows, mod_text[0, r : r + 1], mod_text[1, r : r + 1]
        )
    project_all(image_rows, text_rows, *weights, *outs)


def chunk_at(place, step, flip):
    return (place[0] + Z - step) % Z * X + (place[1] + flip) % X


def project_next(place, p0, p1, p2, p3, mod_image, mod_text, *refs):
    weights, outs, (image_rows, text_rows) = refs[:2], refs[2:6], refs[6:]
    for step, piece in enumerate((p0, p1, p2, p3)):
        for flip in range(X):
            chunk = chunk_at(place, step, flip)
            r = chunk // SLOTS
            image_rows[pl.ds(pl.multiple_of(chunk * PT, PT), PT), :] = normed(
                piece[flip, 0:PT, :].astype(F32),
                mod_image[0, pl.ds(r, 1), :],
                mod_image[1, pl.ds(r, 1), :],
            ).astype(BF16)
            text_rows[pl.ds(pl.multiple_of(chunk * TQ, TQ), TQ), :] = normed(
                piece[flip, PT:ROWS, :].astype(F32),
                mod_text[0, pl.ds(r, 1), :],
                mod_text[1, pl.ds(r, 1), :],
            )
    project_all(image_rows, text_rows, *weights, *outs)


def slot_of(patch, order):
    return sum(jnp.where(patch == order[k], k, 0) for k in range(SLOTS))


def attend(place, order, bias, q_image, q_text, *refs):
    fresh, stale = refs[0:8], refs[8:16]
    out_image, out_text = refs[16:18]
    outs, (o_image, o_text, image, text) = refs[18:26], refs[26:]
    width = q_image.shape[1]
    heads = width // HD
    span, count = SLOTS * PT, SLOTS * TQ
    rows = span + count
    image_keys = len(fresh) * span
    key_count = image_keys + len(fresh) * count
    lane_head = lax.broadcasted_iota(jnp.int32, (rows, width), 1) // HD
    row = lax.broadcasted_iota(jnp.int32, (heads * rows, 1), 0) % rows
    row_slot = jnp.where(row < span, slot_of(row // PT, order), (row - span) // TQ)
    key = lax.broadcasted_iota(jnp.int32, (1, key_count), 1)
    key_slot = jnp.where(
        key < image_keys, slot_of(key % span // PT, order), (key - image_keys) % count // TQ
    )
    is_fresh = key_slot <= row_slot

    def text_of(pieces, r):
        return jnp.concatenate(
            [
                jnp.concatenate(
                    [
                        piece[r, 2 * width + i * count : 2 * width + (i + 1) * count, :]
                        for i in range(2 * width // LANES)
                    ],
                    axis=1,
                )
                for piece in pieces
            ],
            axis=0,
        )

    def scores_of(queries, pieces, text, r):
        keys = jnp.concatenate([piece[r, 0:width, :] for piece in pieces], axis=1)
        return jnp.concatenate([mm(queries, keys), mm_t(queries, text[:, 0:width])], axis=1)

    def summed_of(weights, pieces, text, r):
        values = jnp.concatenate([piece[r, width : 2 * width, :] for piece in pieces], axis=1)
        return mm_t(weights[:, 0:image_keys], values) + mm(
            weights[:, image_keys:], text[:, width:]
        )

    for r in range(REQ):
        q = jnp.concatenate(
            [
                q_image[r * span : (r + 1) * span, :].astype(F32),
                q_text[r * count : (r + 1) * count, :],
            ],
            axis=0,
        )
        queries = jnp.concatenate(
            [jnp.where(lane_head == h, q, 0.0) for h in range(heads)], axis=0
        ).astype(BF16)
        fresh_text, stale_text = text_of(fresh, r), text_of(stale, r)
        scores = jnp.where(
            is_fresh,
            scores_of(queries, fresh, fresh_text, r),
            scores_of(queries, stale, stale_text, r),
        ) * HD ** (-0.5)
        scores = scores + bias[r : r + 1, :]
        top = jnp.max(scores, axis=-1, keepdims=True)
        weights = jnp.exp(scores - top)
        total = jnp.sum(weights, axis=-1, keepdims=True)
        summed = summed_of(
            jnp.where(is_fresh, weights, 0.0).astype(BF16), fresh, fresh_text, r
        ) + summed_of(jnp.where(is_fresh, 0.0, weights).astype(BF16), stale, stale_text, r)
        summed = summed / total
        merged = summed[0:rows]
        for h in range(1, heads):
            merged = jnp.where(lane_head == h, summed[h * rows : (h + 1) * rows], merged)
        o_image[r * span : (r + 1) * span, :] = merged[0:span].astype(BF16)
        o_text[r * count : (r + 1) * count, :] = merged[span:].astype(BF16)
    image[...] = mm(o_image[...], out_image[...])
    text[...] = mm(o_text[...], out_text[...])
    for i, out in enumerate(outs):
        chunk = (place[0] + i // X) % Z * X + (place[1] + i % X) % X
        out[0:PT, :] = image[pl.ds(pl.multiple_of(chunk * PT, PT), PT), :].astype(BF16)
        out[PT:ROWS, :] = text[pl.ds(pl.multiple_of(chunk * TQ, TQ), TQ), :].astype(BF16)


def add_far(p0, p1, p2, p3, out):
    out[...] = summed_parts((p0, p1, p2, p3)).astype(BF16)


def pack_stale(image, text, out):
    width = image.shape[1]
    count = SLOTS * TQ
    for r in range(REQ):
        out[r, 0:width, :] = image[r]
        for i in range(width // LANES):
            out[r, width + i * count : width + (i + 1) * count, :] = text[
                r, :, i * LANES : (i + 1) * LANES
            ]


def own_mod(mod, i, place):
    return mod[i, pl.ds(place[2] // SLOTS, 1), :]


def summed_parts(parts):
    total = parts[0][...].astype(F32)
    for part in parts[1:]:
        total = total + part[...].astype(F32)
    return total


def after_attention(place, rows, p0, p1, p2, p3, p4, mod_image, mod_text, h1, b):
    summed = summed_parts((p0, p1, p2, p3, p4))
    for low, high, mod in ((0, PT, mod_image), (PT, ROWS, mod_text)):
        first = rows[low:high, :].astype(F32) + own_mod(mod, 2, place) * summed[low:high]
        h1[low:high, :] = first
        b[low:high, :] = normed(
            first, own_mod(mod, 3, place), own_mod(mod, 4, place)
        ).astype(BF16)


def feed_forward(place, p0, p1, p2, p3, up_image, down_image, up_text, down_text, *refs):
    outs, (image_rows, text_rows) = refs[:8], refs[8:]
    for d, piece in enumerate((p0, p1, p2, p3)):
        for flip in range(X):
            at = d * X + flip
            image_rows[at * PT : (at + 1) * PT, :] = piece[flip, 0:PT, :]
            text_rows[at * TQ : (at + 1) * TQ, :] = piece[flip, PT:ROWS, :].astype(F32)
    hidden = jax.nn.gelu(mm(image_rows[...], up_image[...]), approximate=True).astype(BF16)
    image = mm(hidden, down_image[...])
    hidden = jax.nn.gelu(
        mm(text_rows[...].astype(BF16), up_text[...]), approximate=True
    ).astype(BF16)
    text = mm(hidden, down_text[...])
    for d in range(Z):
        for flip in range(X):
            at = d * X + flip
            out = outs[(Z - d) % Z * X + flip]
            out[0:PT, :] = image[at * PT : (at + 1) * PT].astype(BF16)
            out[PT:ROWS, :] = text[at * TQ : (at + 1) * TQ].astype(BF16)


def layer_rows(place, h1, parts, mod_image, mod_text):
    summed = summed_parts(parts)
    image = (h1[0:PT, :] + own_mod(mod_image, 5, place) * summed[0:PT]).astype(BF16)
    text = (h1[PT:ROWS, :] + own_mod(mod_text, 5, place) * summed[PT:ROWS]).astype(BF16)
    return image, text


def after_mlp(place, h1, p0, p1, p2, p3, p4, mod_image, mod_text, y):
    image, text = layer_rows(place, h1, (p0, p1, p2, p3, p4), mod_image, mod_text)
    y[0:PT, :] = image
    y[PT:ROWS, :] = text


def last_rows(place, h1, p0, p1, p2, p3, p4, mod_image, mod_text, mod_final, *refs):
    weight, first, out = refs
    image, text = layer_rows(place, h1, (p0, p1, p2, p3, p4), mod_image, mod_text)
    r = place[2] // SLOTS
    rows = normed(
        image.astype(F32), mod_final[pl.ds(r, 1), 0, :], mod_final[pl.ds(r, 1), 1, :]
    ).astype(BF16)
    velocity = mm_t(weight[...], rows)
    width = text.shape[-1]
    text = jnp.where(place[3] == 0, first[PT:ROWS, :].astype(F32), text.astype(F32))
    out[:, 0:width] = text.astype(BF16)
    out[:, width:] = jnp.concatenate(
        [velocity[i * TQ : (i + 1) * TQ] for i in range(velocity.shape[0] // TQ)], axis=1
    ).astype(BF16)


def outputs(place, factor, received, latent, latent_out, text_out):
    width = text_out.shape[-1]
    count = place[3] * CHUNKS
    for chunk in range(CHUNKS):
        text_out[chunk] = received[count + chunk, :, 0:width]
    for r in range(REQ):
        rows = [
            received[CHUNKS + r * SLOTS + p, :, width:].astype(F32) for p in range(SLOTS)
        ]
        for i in range(latent.shape[1] // TQ):
            velocity = jnp.concatenate([each[:, i * PT : (i + 1) * PT] for each in rows], axis=1)
            at = slice(i * TQ, (i + 1) * TQ)
            latent_out[r, at, :] = latent[r, at, :] + factor[r] * velocity


def sigma_of(index_value):
    progress = 1.0 - index_value / STEPS
    return TIME_SHIFT * progress / (1.0 + (TIME_SHIFT - 1.0) * progress)


def on_device(
    hidden_image,
    hidden_text,
    latent,
    timestep,
    text_length,
    text_keep,
    patch_order,
    stale_image_kv,
    stale_text_kv,
    mod_image,
    mod_text,
    mod_final,
    qkv_image,
    out_image,
    up_image,
    down_image,
    qkv_text,
    out_text,
    up_text,
    down_text,
    final_weight,
):
    d_model = hidden_image.shape[2]
    width = qkv_image.shape[3]
    channels = latent.shape[2]
    section = lax.axis_index("section")
    tp = lax.axis_index("tp")
    seq = lax.axis_index("seq")
    place = jnp.stack([tp // X, tp % X, tp, section]).astype(jnp.int32)
    span, count = SLOTS * PT, SLOTS * TQ
    packed_rows = 2 * width + count * 2 * width // LANES
    packed = ((REQ, packed_rows, LANES), BF16)

    stale_image = jnp.transpose(stale_image_kv[0], (0, 2, 3, 1)).reshape(REQ, 2 * width, span)
    stale_text = stale_text_kv[0].reshape(REQ, count, 2 * width)
    (stale,) = call(pack_stale, "pack_stale", [VMEM] * 2, [packed])(stale_image, stale_text)
    stale_pieces = gathered_seq(stale)

    positions = jnp.arange(text_keep.shape[1], dtype=jnp.int32)
    valid = (positions[None, :] < text_length[:, None]) & (text_keep == 1)
    text_bias = jnp.where(valid, 0.0, NEGATIVE).astype(F32).reshape(REQ, Y * C, count)
    piece_seq = [(seq // C + Y - step) % Y * C + (seq + flip) % C for step, flip in PIECES]
    text_bias = jnp.concatenate(
        [lax.dynamic_index_in_dim(text_bias, each, 1, keepdims=False) for each in piece_seq], axis=1
    )
    bias = jnp.concatenate([jnp.zeros((REQ, Y * C * span), F32), text_bias], axis=1)

    def flat_qkv(weight):
        return jnp.transpose(weight[0], (1, 2, 0)).reshape(3 * width, d_model)

    weights = flat_qkv(qkv_image), flat_qkv(qkv_text)
    mods = jnp.transpose(mod_image[0], (1, 0, 2)), jnp.transpose(mod_text[0], (1, 0, 2))

    qkv_shapes = [
        ((CHUNKS * PT, width), BF16),
        ((CHUNKS * TQ, width), F32),
        packed,
        ((CHUNKS * TQ, 2 * width), BF16),
    ]
    rows_scratch = [
        pltpu.VMEM((CHUNKS * PT, d_model), BF16),
        pltpu.VMEM((CHUNKS * TQ, d_model), F32),
    ]
    row_f32, row_bf16 = ((ROWS, d_model), F32), ((ROWS, d_model), BF16)

    def exchanged(parts):
        far = [along_z(parts[step * X + 1], step) for step in RING]
        near = [along_z(parts[step * X], step) for step in RING]
        (half,) = call(add_far, "add_far", [VMEM] * 4, [row_bf16])(parts[1], *far)
        return [parts[0], *near, across_x(half)]

    def rest_of_layer(q_image, q_text, kv, rows):
        partial = call(
            attend,
            "attend",
            [SMEM] * 2 + [VMEM] * 21,
            [row_bf16] * 8,
            [
                pltpu.VMEM((CHUNKS * PT, width), BF16),
                pltpu.VMEM((CHUNKS * TQ, width), BF16),
                pltpu.VMEM((CHUNKS * PT, d_model), F32),
                pltpu.VMEM((CHUNKS * TQ, d_model), F32),
            ],
        )(
            place,
            patch_order,
            bias,
            q_image,
            q_text,
            *gathered_seq(kv),
            *stale_pieces,
            out_image[0],
            out_text[0],
        )
        h1, b = call(
            after_attention, "after_attention", [SMEM] + [VMEM] * 8, [row_f32, row_bf16]
        )(place, rows, *exchanged(partial), *mods)
        pieces = spread_z(jnp.stack([b, across_x(b)]))
        partial = call(
            feed_forward, "feed_forward", [SMEM] + [VMEM] * 8, [row_bf16] * 8, rows_scratch
        )(place, *pieces, up_image[0], down_image[0], up_text[0], down_text[0])
        return h1, exchanged(partial)

    q_image, q_text, kv_first, kv_text_first, own_rows = call(
        project_first,
        "project_first",
        [SMEM] + [VMEM] * 6,
        qkv_shapes + [row_bf16],
        rows_scratch,
        60,
    )(
        place,
        hidden_image.reshape(CHUNKS, PT, d_model),
        hidden_text.reshape(CHUNKS, TQ, d_model),
        *mods,
        *weights,
    )
    h1, received = rest_of_layer(q_image, q_text, kv_first, own_rows)
    (y_first,) = call(after_mlp, "after_mlp", [SMEM] + [VMEM] * 8, [row_bf16])(
        place, h1, *received, *mods
    )
    arrived = to_next_section(y_first, 0)
    pieces = spread_z(jnp.stack([arrived, to_next_section(y_first, 1)]))
    q_image, q_text, kv_next, kv_text_next = call(
        project_next, "project_next", [SMEM] + [VMEM] * 8, qkv_shapes, rows_scratch
    )(place, *pieces, *mods, *weights)
    h1, received = rest_of_layer(q_image, q_text, kv_next, arrived)
    tail = ((TQ, d_model + PT * channels // TQ), BF16)
    (tail_rows,) = call(last_rows, "last_rows", [SMEM] + [VMEM] * 11, [tail])(
        place, h1, *received, *mods, mod_final, jnp.transpose(final_weight), y_first
    )
    shared = lax.all_to_all(
        jnp.broadcast_to(tail_rows[None], (2 * CHUNKS,) + tail_rows.shape),
        ("section", "tp"),
        0,
        0,
        tiled=True,
    )
    index_value = timestep.astype(F32)
    sigma_now = sigma_of(index_value)
    sigma_next = sigma_of(index_value + 1.0)
    factor = jnp.where(section == 0, sigma_next - sigma_now, -sigma_now)
    latent_part, text_hidden = call(
        outputs,
        "outputs",
        [SMEM] * 2 + [VMEM] * 2,
        [((REQ, channels, span), F32), ((CHUNKS, TQ, d_model), BF16)],
    )(place, factor, shared, jnp.transpose(latent, (0, 2, 1)))
    image_kv = jnp.where(section == 0, kv_first[:, : 2 * width], kv_next[:, : 2 * width])
    text_kv = jnp.where(section == 0, kv_text_first, kv_text_next)
    return (
        jnp.transpose(latent_part, (0, 2, 1))[None],
        jnp.transpose(image_kv.reshape(REQ, 2, width, span), (0, 3, 1, 2))[None],
        text_kv.reshape(1, REQ, count, 2, width),
        text_hidden.reshape(1, REQ, count, d_model),
    )


def solution(mesh):
    in_specs = (
        P(None, "seq", None),
        P(None, "seq", None),
        P(None, "seq", None),
        P(),
        P(),
        P(),
        P(),
        P("section", None, "seq", None, "tp"),
        P("section", None, "seq", None, "tp"),
        P("section", None, None, None),
        P("section", None, None, None),
        P(),
        P("section", None, None, "tp"),
        P("section", "tp", None),
        P("section", None, "tp"),
        P("section", "tp", None),
        P("section", None, None, "tp"),
        P("section", "tp", None),
        P("section", None, "tp"),
        P("section", "tp", None),
        P(),
    )
    out_specs = (
        P("section", None, "seq", None),
        P("section", None, "seq", None, "tp"),
        P("section", None, "seq", None, "tp"),
        P("section", None, "seq", None),
    )
    return jax.shard_map(
        on_device, mesh=mesh, in_specs=in_specs, out_specs=out_specs, check_vma=False
    )
```

```python
import jax
import jax.numpy as jnp
from jax import lax
from jax.experimental import pallas as pl
from jax.experimental.pallas import tpu as pltpu
from jax.sharding import PartitionSpec as P

HD = 64
STEPS = 28
EPSILON = 1e-06
NEGATIVE = -1e30
TIME_SHIFT = 3.0

F32 = jnp.float32
BF16 = jnp.bfloat16

REQ, SLOTS, PT, TQ = 2, 4, 32, 8
ROWS = PT + TQ
CHUNKS = REQ * SLOTS
Z, X = 4, 2
Y, C = 4, 2
LANES = 128
RING = (2, 1, 3)
PIECES = ((0, 0), (0, 1), (1, 0), (1, 1), (3, 0), (3, 1), (2, 0), (2, 1))

VMEM = pl.BlockSpec(memory_space=pltpu.VMEM)
SMEM = pl.BlockSpec(memory_space=pltpu.SMEM)


def call(body, name, in_specs, out_shapes, scratch=(), mib=40):
    return pl.pallas_call(
        body,
        name=name,
        in_specs=list(in_specs),
        out_specs=[VMEM] * len(out_shapes),
        out_shape=[jax.ShapeDtypeStruct(*each) for each in out_shapes],
        scratch_shapes=list(scratch),
        compiler_params=pltpu.CompilerParams(vmem_limit_bytes=mib * 1024 * 1024),
    )


def along_z(value, step):
    pairs = [(z * X + x, (z + step) % Z * X + x) for z in range(Z) for x in range(X)]
    return lax.ppermute(value, "tp", pairs)


def across_x(value):
    return lax.ppermute(value, "tp", [(i, i ^ 1) for i in range(Z * X)])


def along_y(value, step):
    pairs = [(y * C + c, (y + step) % Y * C + c) for y in range(Y) for c in range(C)]
    return lax.ppermute(value, "seq", pairs)


def across_core(value):
    return lax.ppermute(value, "seq", [(i, i ^ 1) for i in range(Y * C)])


def to_next_section(value, flip):
    size = Z * X
    return lax.ppermute(value, ("section", "tp"), [(i, size + (i ^ flip)) for i in range(size)])


def gathered_seq(value):
    far = {(0, 0): value, (0, 1): across_core(value)}
    for step in RING:
        far[step, 0] = along_y(value, step)
    for step in RING:
        far[step, 1] = across_core(far[step, 0])
    return [far[piece] for piece in PIECES]


def spread_z(pair):
    received = {step: along_z(pair, step) for step in RING}
    return [pair] + [received[step] for step in (1, 2, 3)]


def normed(rows, shift, scale):
    mean_value = jnp.mean(rows, axis=-1, keepdims=True)
    centred = rows - mean_value
    variance = jnp.mean(centred * centred, axis=-1, keepdims=True)
    return centred * lax.rsqrt(variance + EPSILON) * (1.0 + scale) + shift


def mm(left, right):
    return jnp.dot(left, right, preferred_element_type=F32)


def mm_t(left, right):
    return lax.dot_general(left, right, (((1,), (1,)), ((), ())), preferred_element_type=F32)


def project_all(image_rows, text_rows, w_image, w_text, q_image, q_text, kv, kv_text):
    width = q_image.shape[1]
    image = image_rows[...]
    text = text_rows[...].astype(BF16)
    q_image[...] = mm_t(image, w_image[0:width, :]).astype(BF16)
    q_text[...] = mm_t(text, w_text[0:width, :]).astype(BF16).astype(F32)
    keys_values = mm_t(w_image[width:, :], image).astype(BF16)
    text_kv = mm_t(text, w_text[width:, :]).astype(BF16)
    kv_text[...] = text_kv
    span, count = SLOTS * PT, SLOTS * TQ
    for r in range(REQ):
        kv[r, 0 : 2 * width, :] = keys_values[:, r * span : (r + 1) * span]
        for i in range(2 * width // LANES):
            at = 2 * width + i * count
            kv[r, at : at + count, :] = text_kv[
                r * count : (r + 1) * count, i * LANES : (i + 1) * LANES
            ]


def project_first(place, image, text, mod_image, mod_text, *refs):
    weights, outs, own, (image_rows, text_rows) = refs[:2], refs[2:6], refs[6], refs[7:]
    tp = place[2]
    own[0:PT, :] = image[tp]
    own[PT:ROWS, :] = text[tp]
    for r in range(REQ):
        span, count = SLOTS * PT, SLOTS * TQ
        rows = image[r * SLOTS : (r + 1) * SLOTS].astype(F32).reshape(span, image.shape[2])
        image_rows[r * span : (r + 1) * span, :] = normed(
            rows, mod_image[0, r : r + 1], mod_image[1, r : r + 1]
        ).astype(BF16)
        rows = text[r * SLOTS : (r + 1) * SLOTS].astype(F32).reshape(count, text.shape[2])
        text_rows[r * count : (r + 1) * count, :] = normed(
            rows, mod_text[0, r : r + 1], mod_text[1, r : r + 1]
        )
    project_all(image_rows, text_rows, *weights, *outs)


def chunk_at(place, step, flip):
    return (place[0] + Z - step) % Z * X + (place[1] + flip) % X


def project_next(place, p0, p1, p2, p3, mod_image, mod_text, *refs):
    weights, outs, (image_rows, text_rows) = refs[:2], refs[2:6], refs[6:]
    for step, piece in enumerate((p0, p1, p2, p3)):
        for flip in range(X):
            chunk = chunk_at(place, step, flip)
            r = chunk // SLOTS
            image_rows[pl.ds(pl.multiple_of(chunk * PT, PT), PT), :] = normed(
                piece[flip, 0:PT, :].astype(F32),
                mod_image[0, pl.ds(r, 1), :],
                mod_image[1, pl.ds(r, 1), :],
            ).astype(BF16)
            text_rows[pl.ds(pl.multiple_of(chunk * TQ, TQ), TQ), :] = normed(
                piece[flip, PT:ROWS, :].astype(F32),
                mod_text[0, pl.ds(r, 1), :],
                mod_text[1, pl.ds(r, 1), :],
            )
    project_all(image_rows, text_rows, *weights, *outs)


def slot_of(patch, order):
    return sum(jnp.where(patch == order[k], k, 0) for k in range(SLOTS))


def attend(place, order, bias, q_image, q_text, *refs):
    fresh, stale = refs[0:8], refs[8:16]
    out_image, out_text = refs[16:18]
    outs, (o_image, o_text, image, text) = refs[18:26], refs[26:]
    width = q_image.shape[1]
    heads = width // HD
    span, count = SLOTS * PT, SLOTS * TQ
    rows = span + count
    image_keys = len(fresh) * span
    key_count = image_keys + len(fresh) * count
    lane_head = lax.broadcasted_iota(jnp.int32, (rows, width), 1) // HD
    row = lax.broadcasted_iota(jnp.int32, (heads * rows, 1), 0) % rows
    row_slot = jnp.where(row < span, slot_of(row // PT, order), (row - span) // TQ)
    key = lax.broadcasted_iota(jnp.int32, (1, key_count), 1)
    key_slot = jnp.where(
        key < image_keys, slot_of(key % span // PT, order), (key - image_keys) % count // TQ
    )
    is_fresh = key_slot <= row_slot

    def text_of(pieces, r):
        return jnp.concatenate(
            [
                jnp.concatenate(
                    [
                        piece[r, 2 * width + i * count : 2 * width + (i + 1) * count, :]
                        for i in range(2 * width // LANES)
                    ],
                    axis=1,
                )
                for piece in pieces
            ],
            axis=0,
        )

    def scores_of(queries, pieces, text, r):
        keys = jnp.concatenate([piece[r, 0:width, :] for piece in pieces], axis=1)
        return jnp.concatenate([mm(queries, keys), mm_t(queries, text[:, 0:width])], axis=1)

    def summed_of(weights, pieces, text, r):
        values = jnp.concatenate([piece[r, width : 2 * width, :] for piece in pieces], axis=1)
        return mm_t(weights[:, 0:image_keys], values) + mm(
            weights[:, image_keys:], text[:, width:]
        )

    for r in range(REQ):
        q = jnp.concatenate(
            [
                q_image[r * span : (r + 1) * span, :].astype(F32),
                q_text[r * count : (r + 1) * count, :],
            ],
            axis=0,
        )
        queries = jnp.concatenate(
            [jnp.where(lane_head == h, q, 0.0) for h in range(heads)], axis=0
        ).astype(BF16)
        fresh_text, stale_text = text_of(fresh, r), text_of(stale, r)
        scores = jnp.where(
            is_fresh,
            scores_of(queries, fresh, fresh_text, r),
            scores_of(queries, stale, stale_text, r),
        ) * HD ** (-0.5)
        scores = scores + bias[r : r + 1, :]
        top = jnp.max(scores, axis=-1, keepdims=True)
        weights = jnp.exp(scores - top)
        total = jnp.sum(weights, axis=-1, keepdims=True)
        summed = summed_of(
            jnp.where(is_fresh, weights, 0.0).astype(BF16), fresh, fresh_text, r
        ) + summed_of(jnp.where(is_fresh, 0.0, weights).astype(BF16), stale, stale_text, r)
        summed = summed / total
        merged = summed[0:rows]
        for h in range(1, heads):
            merged = jnp.where(lane_head == h, summed[h * rows : (h + 1) * rows], merged)
        o_image[r * span : (r + 1) * span, :] = merged[0:span].astype(BF16)
        o_text[r * count : (r + 1) * count, :] = merged[span:].astype(BF16)
    image[...] = mm(o_image[...], out_image[...])
    text[...] = mm(o_text[...], out_text[...])
    for i, out in enumerate(outs):
        chunk = (place[0] + i // X) % Z * X + (place[1] + i % X) % X
        out[0:PT, :] = image[pl.ds(pl.multiple_of(chunk * PT, PT), PT), :].astype(BF16)
        out[PT:ROWS, :] = text[pl.ds(pl.multiple_of(chunk * TQ, TQ), TQ), :].astype(BF16)


def add_far(p0, p1, p2, p3, out):
    out[...] = summed_parts((p0, p1, p2, p3)).astype(BF16)


def pack_stale(image, text, out):
    width = image.shape[1]
    count = SLOTS * TQ
    for r in range(REQ):
        out[r, 0:width, :] = image[r]
        for i in range(width // LANES):
            out[r, width + i * count : width + (i + 1) * count, :] = text[
                r, :, i * LANES : (i + 1) * LANES
            ]


def own_mod(mod, i, place):
    return mod[i, pl.ds(place[2] // SLOTS, 1), :]


def summed_parts(parts):
    total = parts[0][...].astype(F32)
    for part in parts[1:]:
        total = total + part[...].astype(F32)
    return total


def after_attention(place, rows, p0, p1, p2, p3, p4, mod_image, mod_text, h1, b):
    summed = summed_parts((p0, p1, p2, p3, p4))
    for low, high, mod in ((0, PT, mod_image), (PT, ROWS, mod_text)):
        first = rows[low:high, :].astype(F32) + own_mod(mod, 2, place) * summed[low:high]
        h1[low:high, :] = first
        b[low:high, :] = normed(
            first, own_mod(mod, 3, place), own_mod(mod, 4, place)
        ).astype(BF16)


def feed_forward(place, p0, p1, p2, p3, up_image, down_image, up_text, down_text, *refs):
    outs, (image_rows, text_rows, image_hidden, text_hidden) = refs[:8], refs[8:]
    for d, piece in enumerate((p0, p1, p2, p3)):
        for flip in range(X):
            at = d * X + flip
            image_rows[at * PT : (at + 1) * PT, :] = piece[flip, 0:PT, :]
            text_rows[at * TQ : (at + 1) * TQ, :] = piece[flip, PT:ROWS, :].astype(F32)
    hidden_width, d_model = down_image.shape
    block = hidden_width // 3

    @pl.loop(0, hidden_width // block)
    def _(j):
        lanes = pl.ds(pl.multiple_of(j * block, block), block)
        for rows, up, hidden in (
            (image_rows, up_image, image_hidden),
            (text_rows, up_text, text_hidden),
        ):
            hidden[:, lanes] = jax.nn.gelu(
                mm(rows[...].astype(BF16), up[:, lanes]), approximate=True
            ).astype(BF16)

    wide = d_model // 3

    @pl.loop(0, d_model // wide)
    def _(j):
        lanes = pl.ds(pl.multiple_of(j * wide, wide), wide)
        image = mm(image_hidden[...], down_image[:, lanes])
        text = mm(text_hidden[...], down_text[:, lanes])
        for d in range(Z):
            for flip in range(X):
                at = d * X + flip
                out = outs[(Z - d) % Z * X + flip]
                out[0:PT, lanes] = image[at * PT : (at + 1) * PT].astype(BF16)
                out[PT:ROWS, lanes] = text[at * TQ : (at + 1) * TQ].astype(BF16)


def layer_rows(place, h1, parts, mod_image, mod_text):
    summed = summed_parts(parts)
    image = (h1[0:PT, :] + own_mod(mod_image, 5, place) * summed[0:PT]).astype(BF16)
    text = (h1[PT:ROWS, :] + own_mod(mod_text, 5, place) * summed[PT:ROWS]).astype(BF16)
    return image, text


def after_mlp(place, h1, p0, p1, p2, p3, p4, mod_image, mod_text, y):
    image, text = layer_rows(place, h1, (p0, p1, p2, p3, p4), mod_image, mod_text)
    y[0:PT, :] = image
    y[PT:ROWS, :] = text


def last_rows(place, h1, p0, p1, p2, p3, p4, mod_image, mod_text, mod_final, *refs):
    weight, first, out = refs
    image, text = layer_rows(place, h1, (p0, p1, p2, p3, p4), mod_image, mod_text)
    r = place[2] // SLOTS
    rows = normed(
        image.astype(F32), mod_final[pl.ds(r, 1), 0, :], mod_final[pl.ds(r, 1), 1, :]
    ).astype(BF16)
    velocity = mm_t(weight[...], rows)
    width = text.shape[-1]
    text = jnp.where(place[3] == 0, first[PT:ROWS, :].astype(F32), text.astype(F32))
    out[:, 0:width] = text.astype(BF16)
    out[:, width:] = jnp.concatenate(
        [velocity[i * TQ : (i + 1) * TQ] for i in range(velocity.shape[0] // TQ)], axis=1
    ).astype(BF16)


def outputs(place, factor, received, latent, latent_out, text_out):
    width = text_out.shape[-1]
    count = place[3] * CHUNKS
    for chunk in range(CHUNKS):
        text_out[chunk] = received[count + chunk, :, 0:width]
    for r in range(REQ):
        rows = [
            received[CHUNKS + r * SLOTS + p, :, width:].astype(F32) for p in range(SLOTS)
        ]
        for i in range(latent.shape[1] // TQ):
            velocity = jnp.concatenate([each[:, i * PT : (i + 1) * PT] for each in rows], axis=1)
            at = slice(i * TQ, (i + 1) * TQ)
            latent_out[r, at, :] = latent[r, at, :] + factor[r] * velocity


def sigma_of(index_value):
    progress = 1.0 - index_value / STEPS
    return TIME_SHIFT * progress / (1.0 + (TIME_SHIFT - 1.0) * progress)


def on_device(
    hidden_image,
    hidden_text,
    latent,
    timestep,
    text_length,
    text_keep,
    patch_order,
    stale_image_kv,
    stale_text_kv,
    mod_image,
    mod_text,
    mod_final,
    qkv_image,
    out_image,
    up_image,
    down_image,
    qkv_text,
    out_text,
    up_text,
    down_text,
    final_weight,
):
    d_model = hidden_image.shape[2]
    width = qkv_image.shape[3]
    channels = latent.shape[2]
    section = lax.axis_index("section")
    tp = lax.axis_index("tp")
    seq = lax.axis_index("seq")
    place = jnp.stack([tp // X, tp % X, tp, section]).astype(jnp.int32)
    span, count = SLOTS * PT, SLOTS * TQ
    packed_rows = 2 * width + count * 2 * width // LANES
    packed = ((REQ, packed_rows, LANES), BF16)

    stale_image = jnp.transpose(stale_image_kv[0], (0, 2, 3, 1)).reshape(REQ, 2 * width, span)
    stale_text = stale_text_kv[0].reshape(REQ, count, 2 * width)
    (stale,) = call(pack_stale, "pack_stale", [VMEM] * 2, [packed])(stale_image, stale_text)
    stale_pieces = gathered_seq(stale)

    positions = jnp.arange(text_keep.shape[1], dtype=jnp.int32)
    valid = (positions[None, :] < text_length[:, None]) & (text_keep == 1)
    text_bias = jnp.where(valid, 0.0, NEGATIVE).astype(F32).reshape(REQ, Y * C, count)
    piece_seq = [(seq // C + Y - step) % Y * C + (seq + flip) % C for step, flip in PIECES]
    text_bias = jnp.concatenate(
        [lax.dynamic_index_in_dim(text_bias, each, 1, keepdims=False) for each in piece_seq], axis=1
    )
    bias = jnp.concatenate([jnp.zeros((REQ, Y * C * span), F32), text_bias], axis=1)

    def flat_qkv(weight):
        return jnp.transpose(weight[0], (1, 2, 0)).reshape(3 * width, d_model)

    weights = flat_qkv(qkv_image), flat_qkv(qkv_text)
    mods = jnp.transpose(mod_image[0], (1, 0, 2)), jnp.transpose(mod_text[0], (1, 0, 2))

    qkv_shapes = [
        ((CHUNKS * PT, width), BF16),
        ((CHUNKS * TQ, width), F32),
        packed,
        ((CHUNKS * TQ, 2 * width), BF16),
    ]
    rows_scratch = [
        pltpu.VMEM((CHUNKS * PT, d_model), BF16),
        pltpu.VMEM((CHUNKS * TQ, d_model), F32),
    ]
    row_f32, row_bf16 = ((ROWS, d_model), F32), ((ROWS, d_model), BF16)

    def exchanged(parts):
        far = [along_z(parts[step * X + 1], step) for step in RING]
        near = [along_z(parts[step * X], step) for step in RING]
        (half,) = call(add_far, "add_far", [VMEM] * 4, [row_bf16])(parts[1], *far)
        return [parts[0], *near, across_x(half)]

    def rest_of_layer(q_image, q_text, kv, rows):
        partial = call(
            attend,
            "attend",
            [SMEM] * 2 + [VMEM] * 21,
            [row_bf16] * 8,
            [
                pltpu.VMEM((CHUNKS * PT, width), BF16),
                pltpu.VMEM((CHUNKS * TQ, width), BF16),
                pltpu.VMEM((CHUNKS * PT, d_model), F32),
                pltpu.VMEM((CHUNKS * TQ, d_model), F32),
            ],
        )(
            place,
            patch_order,
            bias,
            q_image,
            q_text,
            *gathered_seq(kv),
            *stale_pieces,
            out_image[0],
            out_text[0],
        )
        h1, b = call(
            after_attention, "after_attention", [SMEM] + [VMEM] * 8, [row_f32, row_bf16]
        )(place, rows, *exchanged(partial), *mods)
        pieces = spread_z(jnp.stack([b, across_x(b)]))
        partial = call(
            feed_forward,
            "feed_forward",
            [SMEM] + [VMEM] * 8,
            [row_bf16] * 8,
            rows_scratch
            + [
                pltpu.VMEM((CHUNKS * PT, up_image.shape[2]), BF16),
                pltpu.VMEM((CHUNKS * TQ, up_image.shape[2]), BF16),
            ],
        )(place, *pieces, up_image[0], down_image[0], up_text[0], down_text[0])
        return h1, exchanged(partial)

    q_image, q_text, kv_first, kv_text_first, own_rows = call(
        project_first,
        "project_first",
        [SMEM] + [VMEM] * 6,
        qkv_shapes + [row_bf16],
        rows_scratch,
        60,
    )(
        place,
        hidden_image.reshape(CHUNKS, PT, d_model),
        hidden_text.reshape(CHUNKS, TQ, d_model),
        *mods,
        *weights,
    )
    h1, received = rest_of_layer(q_image, q_text, kv_first, own_rows)
    (y_first,) = call(after_mlp, "after_mlp", [SMEM] + [VMEM] * 8, [row_bf16])(
        place, h1, *received, *mods
    )
    arrived = to_next_section(y_first, 0)
    pieces = spread_z(jnp.stack([arrived, to_next_section(y_first, 1)]))
    q_image, q_text, kv_next, kv_text_next = call(
        project_next, "project_next", [SMEM] + [VMEM] * 8, qkv_shapes, rows_scratch
    )(place, *pieces, *mods, *weights)
    h1, received = rest_of_layer(q_image, q_text, kv_next, arrived)
    tail = ((TQ, d_model + PT * channels // TQ), BF16)
    (tail_rows,) = call(last_rows, "last_rows", [SMEM] + [VMEM] * 11, [tail])(
        place, h1, *received, *mods, mod_final, jnp.transpose(final_weight), y_first
    )
    shared = lax.all_to_all(
        jnp.broadcast_to(tail_rows[None], (2 * CHUNKS,) + tail_rows.shape),
        ("section", "tp"),
        0,
        0,
        tiled=True,
    )
    index_value = timestep.astype(F32)
    sigma_now = sigma_of(index_value)
    sigma_next = sigma_of(index_value + 1.0)
    factor = jnp.where(section == 0, sigma_next - sigma_now, -sigma_now)
    latent_part, text_hidden = call(
        outputs,
        "outputs",
        [SMEM] * 2 + [VMEM] * 2,
        [((REQ, channels, span), F32), ((CHUNKS, TQ, d_model), BF16)],
    )(place, factor, shared, jnp.transpose(latent, (0, 2, 1)))
    image_kv = jnp.where(section == 0, kv_first[:, : 2 * width], kv_next[:, : 2 * width])
    text_kv = jnp.where(section == 0, kv_text_first, kv_text_next)
    return (
        jnp.transpose(latent_part, (0, 2, 1))[None],
        jnp.transpose(image_kv.reshape(REQ, 2, width, span), (0, 3, 1, 2))[None],
        text_kv.reshape(1, REQ, count, 2, width),
        text_hidden.reshape(1, REQ, count, d_model),
    )


def solution(mesh):
    in_specs = (
        P(None, "seq", None),
        P(None, "seq", None),
        P(None, "seq", None),
        P(),
        P(),
        P(),
        P(),
        P("section", None, "seq", None, "tp"),
        P("section", None, "seq", None, "tp"),
        P("section", None, None, None),
        P("section", None, None, None),
        P(),
        P("section", None, None, "tp"),
        P("section", "tp", None),
        P("section", None, "tp"),
        P("section", "tp", None),
        P("section", None, None, "tp"),
        P("section", "tp", None),
        P("section", None, "tp"),
        P("section", "tp", None),
        P(),
    )
    out_specs = (
        P("section", None, "seq", None),
        P("section", None, "seq", None, "tp"),
        P("section", None, "seq", None, "tp"),
        P("section", None, "seq", None),
    )
    return jax.shard_map(
        on_device, mesh=mesh, in_specs=in_specs, out_specs=out_specs, check_vma=False
    )
```

```python
import jax
import jax.numpy as jnp
from jax import lax
from jax.experimental import pallas as pl
from jax.experimental.pallas import tpu as pltpu
from jax.sharding import PartitionSpec as P

HD = 64
STEPS = 28
EPSILON = 1e-06
NEGATIVE = -1e30
TIME_SHIFT = 3.0

F32 = jnp.float32
BF16 = jnp.bfloat16

REQ, SLOTS, PT, TQ = 2, 4, 32, 8
ROWS = PT + TQ
CHUNKS = REQ * SLOTS
Z, X = 4, 2
Y, C = 4, 2
LANES = 128
RING = (2, 1, 3)
PIECES = ((0, 0), (0, 1), (1, 0), (1, 1), (3, 0), (3, 1), (2, 0), (2, 1))

VMEM = pl.BlockSpec(memory_space=pltpu.VMEM)
SMEM = pl.BlockSpec(memory_space=pltpu.SMEM)


def call(body, name, in_specs, out_shapes, scratch=(), mib=40):
    return pl.pallas_call(
        body,
        name=name,
        in_specs=list(in_specs),
        out_specs=[VMEM] * len(out_shapes),
        out_shape=[jax.ShapeDtypeStruct(*each) for each in out_shapes],
        scratch_shapes=list(scratch),
        compiler_params=pltpu.CompilerParams(vmem_limit_bytes=mib * 1024 * 1024),
    )


def along_z(value, step):
    pairs = [(z * X + x, (z + step) % Z * X + x) for z in range(Z) for x in range(X)]
    return lax.ppermute(value, "tp", pairs)


def across_x(value):
    return lax.ppermute(value, "tp", [(i, i ^ 1) for i in range(Z * X)])


def along_y(value, step):
    pairs = [(y * C + c, (y + step) % Y * C + c) for y in range(Y) for c in range(C)]
    return lax.ppermute(value, "seq", pairs)


def across_core(value):
    return lax.ppermute(value, "seq", [(i, i ^ 1) for i in range(Y * C)])


def to_next_section(value, flip):
    size = Z * X
    return lax.ppermute(value, ("section", "tp"), [(i, size + (i ^ flip)) for i in range(size)])


def gathered_seq(value):
    far = {(0, 0): value, (0, 1): across_core(value)}
    for step in RING:
        far[step, 0] = along_y(value, step)
    for step in RING:
        far[step, 1] = across_core(far[step, 0])
    return [far[piece] for piece in PIECES]


def spread_z(pair):
    received = {step: along_z(pair, step) for step in RING}
    return [pair] + [received[step] for step in (1, 2, 3)]


def normed(rows, shift, scale):
    mean_value = jnp.mean(rows, axis=-1, keepdims=True)
    centred = rows - mean_value
    variance = jnp.mean(centred * centred, axis=-1, keepdims=True)
    return centred * lax.rsqrt(variance + EPSILON) * (1.0 + scale) + shift


def mm(left, right):
    return jnp.dot(left, right, preferred_element_type=F32)


def mm_t(left, right):
    return lax.dot_general(left, right, (((1,), (1,)), ((), ())), preferred_element_type=F32)


def project_all(image_rows, text_rows, w_image, w_text, q_image, q_text, kv, kv_text):
    width = q_image.shape[1]
    image = image_rows[...]
    text = text_rows[...].astype(BF16)
    q_image[...] = mm_t(image, w_image[0:width, :]).astype(BF16)
    q_text[...] = mm_t(text, w_text[0:width, :]).astype(BF16).astype(F32)
    keys_values = mm_t(w_image[width:, :], image).astype(BF16)
    text_kv = mm_t(text, w_text[width:, :]).astype(BF16)
    kv_text[...] = text_kv
    span, count = SLOTS * PT, SLOTS * TQ
    for r in range(REQ):
        kv[r, 0 : 2 * width, :] = keys_values[:, r * span : (r + 1) * span]
        for i in range(2 * width // LANES):
            at = 2 * width + i * count
            kv[r, at : at + count, :] = text_kv[
                r * count : (r + 1) * count, i * LANES : (i + 1) * LANES
            ]


def project_first(place, image, text, mod_image, mod_text, *refs):
    weights, outs, own, (image_rows, text_rows) = refs[:2], refs[2:6], refs[6], refs[7:]
    tp = place[2]
    own[0:PT, :] = image[tp]
    own[PT:ROWS, :] = text[tp]
    for r in range(REQ):
        span, count = SLOTS * PT, SLOTS * TQ
        rows = image[r * SLOTS : (r + 1) * SLOTS].astype(F32).reshape(span, image.shape[2])
        image_rows[r * span : (r + 1) * span, :] = normed(
            rows, mod_image[0, r : r + 1], mod_image[1, r : r + 1]
        ).astype(BF16)
        rows = text[r * SLOTS : (r + 1) * SLOTS].astype(F32).reshape(count, text.shape[2])
        text_rows[r * count : (r + 1) * count, :] = normed(
            rows, mod_text[0, r : r + 1], mod_text[1, r : r + 1]
        )
    project_all(image_rows, text_rows, *weights, *outs)


def chunk_at(place, step, flip):
    return (place[0] + Z - step) % Z * X + (place[1] + flip) % X


def project_next(place, p0, p1, p2, p3, mod_image, mod_text, *refs):
    weights, outs, (image_rows, text_rows) = refs[:2], refs[2:6], refs[6:]
    for step, piece in enumerate((p0, p1, p2, p3)):
        for flip in range(X):
            chunk = chunk_at(place, step, flip)
            r = chunk // SLOTS
            image_rows[pl.ds(pl.multiple_of(chunk * PT, PT), PT), :] = normed(
                piece[flip, 0:PT, :].astype(F32),
                mod_image[0, pl.ds(r, 1), :],
                mod_image[1, pl.ds(r, 1), :],
            ).astype(BF16)
            text_rows[pl.ds(pl.multiple_of(chunk * TQ, TQ), TQ), :] = normed(
                piece[flip, PT:ROWS, :].astype(F32),
                mod_text[0, pl.ds(r, 1), :],
                mod_text[1, pl.ds(r, 1), :],
            )
    project_all(image_rows, text_rows, *weights, *outs)


def slot_of(patch, order):
    return sum(jnp.where(patch == order[k], k, 0) for k in range(SLOTS))


def attend(place, order, bias, q_image, q_text, *refs):
    fresh, stale = refs[0:8], refs[8:16]
    out_image, out_text = refs[16:18]
    outs, (o_image, o_text, image, text) = refs[18:26], refs[26:]
    width = q_image.shape[1]
    heads = width // HD
    span, count = SLOTS * PT, SLOTS * TQ
    rows = span + count
    image_keys = len(fresh) * span
    key_count = image_keys + len(fresh) * count
    lane_head = lax.broadcasted_iota(jnp.int32, (rows, width), 1) // HD
    row = lax.broadcasted_iota(jnp.int32, (heads * rows, 1), 0) % rows
    row_slot = jnp.where(row < span, slot_of(row // PT, order), (row - span) // TQ)
    key = lax.broadcasted_iota(jnp.int32, (1, key_count), 1)
    key_slot = jnp.where(
        key < image_keys, slot_of(key % span // PT, order), (key - image_keys) % count // TQ
    )
    is_fresh = key_slot <= row_slot

    def text_of(pieces, r):
        return jnp.concatenate(
            [
                jnp.concatenate(
                    [
                        piece[r, 2 * width + i * count : 2 * width + (i + 1) * count, :]
                        for i in range(2 * width // LANES)
                    ],
                    axis=1,
                )
                for piece in pieces
            ],
            axis=0,
        )

    fresh_share = jnp.where(is_fresh, 1.0, 0.0).astype(BF16)

    def all_of(pieces, r, at):
        return jnp.concatenate([piece[r, at : at + width, :] for piece in pieces], axis=1)

    for r in range(REQ):
        q = jnp.concatenate(
            [
                q_image[r * span : (r + 1) * span, :].astype(F32),
                q_text[r * count : (r + 1) * count, :],
            ],
            axis=0,
        )
        q = q * HD ** (-0.5)
        queries = jnp.concatenate(
            [jnp.where(lane_head == h, q, 0.0) for h in range(heads)], axis=0
        ).astype(BF16)
        fresh_text, stale_text = text_of(fresh, r), text_of(stale, r)
        image_scores = jnp.where(
            is_fresh[:, 0:image_keys],
            mm(queries, all_of(fresh, r, 0)),
            mm(queries, all_of(stale, r, 0)),
        )
        text_scores = jnp.where(
            is_fresh[:, image_keys:],
            mm_t(queries, fresh_text[:, 0:width]),
            mm_t(queries, stale_text[:, 0:width]),
        ) + bias[r : r + 1, image_keys:]
        top = jnp.maximum(
            jnp.max(image_scores, axis=-1, keepdims=True),
            jnp.max(text_scores, axis=-1, keepdims=True),
        )
        image_weights = jnp.exp(image_scores - top)
        text_weights = jnp.exp(text_scores - top)
        total = jnp.sum(image_weights, axis=-1, keepdims=True) + jnp.sum(
            text_weights, axis=-1, keepdims=True
        )
        whole = image_weights.astype(BF16)
        part = whole * fresh_share[:, 0:image_keys]
        summed = mm_t(part, all_of(fresh, r, width)) + mm_t(
            whole - part, all_of(stale, r, width)
        )
        whole = text_weights.astype(BF16)
        part = whole * fresh_share[:, image_keys:]
        summed = (
            summed
            + mm(part, fresh_text[:, width:])
            + mm(whole - part, stale_text[:, width:])
        )
        summed = summed / total
        merged = summed[0:rows]
        for h in range(1, heads):
            merged = jnp.where(lane_head == h, summed[h * rows : (h + 1) * rows], merged)
        o_image[r * span : (r + 1) * span, :] = merged[0:span].astype(BF16)
        o_text[r * count : (r + 1) * count, :] = merged[span:].astype(BF16)
    image[...] = mm(o_image[...], out_image[...])
    text[...] = mm(o_text[...], out_text[...])
    for i, out in enumerate(outs):
        chunk = (place[0] + i // X) % Z * X + (place[1] + i % X) % X
        out[0:PT, :] = image[pl.ds(pl.multiple_of(chunk * PT, PT), PT), :].astype(BF16)
        out[PT:ROWS, :] = text[pl.ds(pl.multiple_of(chunk * TQ, TQ), TQ), :].astype(BF16)


def add_far(p0, p1, p2, p3, out):
    out[...] = summed_parts((p0, p1, p2, p3)).astype(BF16)


def pack_stale(image, text, out):
    width = image.shape[1]
    count = SLOTS * TQ
    for r in range(REQ):
        out[r, 0:width, :] = image[r]
        for i in range(width // LANES):
            out[r, width + i * count : width + (i + 1) * count, :] = text[
                r, :, i * LANES : (i + 1) * LANES
            ]


def own_mod(mod, i, place):
    return mod[i, pl.ds(place[2] // SLOTS, 1), :]


def summed_parts(parts):
    total = parts[0][...].astype(F32)
    for part in parts[1:]:
        total = total + part[...].astype(F32)
    return total


def after_attention(place, rows, p0, p1, p2, p3, p4, mod_image, mod_text, h1, b):
    summed = summed_parts((p0, p1, p2, p3, p4))
    for low, high, mod in ((0, PT, mod_image), (PT, ROWS, mod_text)):
        first = rows[low:high, :].astype(F32) + own_mod(mod, 2, place) * summed[low:high]
        h1[low:high, :] = first
        b[low:high, :] = normed(
            first, own_mod(mod, 3, place), own_mod(mod, 4, place)
        ).astype(BF16)


def feed_forward(place, p0, p1, p2, p3, up_image, down_image, up_text, down_text, *refs):
    outs, (image_rows, text_rows, image_hidden, text_hidden) = refs[:8], refs[8:]
    for d, piece in enumerate((p0, p1, p2, p3)):
        for flip in range(X):
            at = d * X + flip
            image_rows[at * PT : (at + 1) * PT, :] = piece[flip, 0:PT, :]
            text_rows[at * TQ : (at + 1) * TQ, :] = piece[flip, PT:ROWS, :].astype(F32)
    hidden_width, d_model = down_image.shape
    block = hidden_width // 3

    @pl.loop(0, hidden_width // block)
    def _(j):
        lanes = pl.ds(pl.multiple_of(j * block, block), block)
        for rows, up, hidden in (
            (image_rows, up_image, image_hidden),
            (text_rows, up_text, text_hidden),
        ):
            hidden[:, lanes] = jax.nn.gelu(
                mm(rows[...].astype(BF16), up[:, lanes]), approximate=True
            ).astype(BF16)

    wide = d_model // 3

    @pl.loop(0, d_model // wide)
    def _(j):
        lanes = pl.ds(pl.multiple_of(j * wide, wide), wide)
        image = mm(image_hidden[...], down_image[:, lanes])
        text = mm(text_hidden[...], down_text[:, lanes])
        for d in range(Z):
            for flip in range(X):
                at = d * X + flip
                out = outs[(Z - d) % Z * X + flip]
                out[0:PT, lanes] = image[at * PT : (at + 1) * PT].astype(BF16)
                out[PT:ROWS, lanes] = text[at * TQ : (at + 1) * TQ].astype(BF16)


def layer_rows(place, h1, parts, mod_image, mod_text):
    summed = summed_parts(parts)
    image = (h1[0:PT, :] + own_mod(mod_image, 5, place) * summed[0:PT]).astype(BF16)
    text = (h1[PT:ROWS, :] + own_mod(mod_text, 5, place) * summed[PT:ROWS]).astype(BF16)
    return image, text


def after_mlp(place, h1, p0, p1, p2, p3, p4, mod_image, mod_text, y):
    image, text = layer_rows(place, h1, (p0, p1, p2, p3, p4), mod_image, mod_text)
    y[0:PT, :] = image
    y[PT:ROWS, :] = text


def last_rows(place, h1, p0, p1, p2, p3, p4, mod_image, mod_text, mod_final, *refs):
    weight, first, out = refs
    image, text = layer_rows(place, h1, (p0, p1, p2, p3, p4), mod_image, mod_text)
    r = place[2] // SLOTS
    rows = normed(
        image.astype(F32), mod_final[pl.ds(r, 1), 0, :], mod_final[pl.ds(r, 1), 1, :]
    ).astype(BF16)
    velocity = mm_t(weight[...], rows)
    width = text.shape[-1]
    text = jnp.where(place[3] == 0, first[PT:ROWS, :].astype(F32), text.astype(F32))
    out[:, 0:width] = text.astype(BF16)
    out[:, width:] = jnp.concatenate(
        [velocity[i * TQ : (i + 1) * TQ] for i in range(velocity.shape[0] // TQ)], axis=1
    ).astype(BF16)


def outputs(place, factor, received, latent, latent_out, text_out):
    width = text_out.shape[-1]
    count = place[3] * CHUNKS
    for chunk in range(CHUNKS):
        text_out[chunk] = received[count + chunk, :, 0:width]
    for r in range(REQ):
        rows = [
            received[CHUNKS + r * SLOTS + p, :, width:].astype(F32) for p in range(SLOTS)
        ]
        for i in range(latent.shape[1] // TQ):
            velocity = jnp.concatenate([each[:, i * PT : (i + 1) * PT] for each in rows], axis=1)
            at = slice(i * TQ, (i + 1) * TQ)
            latent_out[r, at, :] = latent[r, at, :] + factor[r] * velocity


def sigma_of(index_value):
    progress = 1.0 - index_value / STEPS
    return TIME_SHIFT * progress / (1.0 + (TIME_SHIFT - 1.0) * progress)


def on_device(
    hidden_image,
    hidden_text,
    latent,
    timestep,
    text_length,
    text_keep,
    patch_order,
    stale_image_kv,
    stale_text_kv,
    mod_image,
    mod_text,
    mod_final,
    qkv_image,
    out_image,
    up_image,
    down_image,
    qkv_text,
    out_text,
    up_text,
    down_text,
    final_weight,
):
    d_model = hidden_image.shape[2]
    width = qkv_image.shape[3]
    channels = latent.shape[2]
    section = lax.axis_index("section")
    tp = lax.axis_index("tp")
    seq = lax.axis_index("seq")
    place = jnp.stack([tp // X, tp % X, tp, section]).astype(jnp.int32)
    span, count = SLOTS * PT, SLOTS * TQ
    packed_rows = 2 * width + count * 2 * width // LANES
    packed = ((REQ, packed_rows, LANES), BF16)

    stale_image = jnp.transpose(stale_image_kv[0], (0, 2, 3, 1)).reshape(REQ, 2 * width, span)
    stale_text = stale_text_kv[0].reshape(REQ, count, 2 * width)
    (stale,) = call(pack_stale, "pack_stale", [VMEM] * 2, [packed])(stale_image, stale_text)
    stale_pieces = gathered_seq(stale)

    positions = jnp.arange(text_keep.shape[1], dtype=jnp.int32)
    valid = (positions[None, :] < text_length[:, None]) & (text_keep == 1)
    text_bias = jnp.where(valid, 0.0, NEGATIVE).astype(F32).reshape(REQ, Y * C, count)
    piece_seq = [(seq // C + Y - step) % Y * C + (seq + flip) % C for step, flip in PIECES]
    text_bias = jnp.concatenate(
        [lax.dynamic_index_in_dim(text_bias, each, 1, keepdims=False) for each in piece_seq], axis=1
    )
    bias = jnp.concatenate([jnp.zeros((REQ, Y * C * span), F32), text_bias], axis=1)

    def flat_qkv(weight):
        return jnp.transpose(weight[0], (1, 2, 0)).reshape(3 * width, d_model)

    weights = flat_qkv(qkv_image), flat_qkv(qkv_text)
    mods = jnp.transpose(mod_image[0], (1, 0, 2)), jnp.transpose(mod_text[0], (1, 0, 2))

    qkv_shapes = [
        ((CHUNKS * PT, width), BF16),
        ((CHUNKS * TQ, width), F32),
        packed,
        ((CHUNKS * TQ, 2 * width), BF16),
    ]
    rows_scratch = [
        pltpu.VMEM((CHUNKS * PT, d_model), BF16),
        pltpu.VMEM((CHUNKS * TQ, d_model), F32),
    ]
    row_f32, row_bf16 = ((ROWS, d_model), F32), ((ROWS, d_model), BF16)

    def exchanged(parts):
        far = [along_z(parts[step * X + 1], step) for step in RING]
        near = [along_z(parts[step * X], step) for step in RING]
        (half,) = call(add_far, "add_far", [VMEM] * 4, [row_bf16])(parts[1], *far)
        return [parts[0], *near, across_x(half)]

    def rest_of_layer(q_image, q_text, kv, rows):
        partial = call(
            attend,
            "attend",
            [SMEM] * 2 + [VMEM] * 21,
            [row_bf16] * 8,
            [
                pltpu.VMEM((CHUNKS * PT, width), BF16),
                pltpu.VMEM((CHUNKS * TQ, width), BF16),
                pltpu.VMEM((CHUNKS * PT, d_model), F32),
                pltpu.VMEM((CHUNKS * TQ, d_model), F32),
            ],
        )(
            place,
            patch_order,
            bias,
            q_image,
            q_text,
            *gathered_seq(kv),
            *stale_pieces,
            out_image[0],
            out_text[0],
        )
        h1, b = call(
            after_attention, "after_attention", [SMEM] + [VMEM] * 8, [row_f32, row_bf16]
        )(place, rows, *exchanged(partial), *mods)
        pieces = spread_z(jnp.stack([b, across_x(b)]))
        partial = call(
            feed_forward,
            "feed_forward",
            [SMEM] + [VMEM] * 8,
            [row_bf16] * 8,
            rows_scratch
            + [
                pltpu.VMEM((CHUNKS * PT, up_image.shape[2]), BF16),
                pltpu.VMEM((CHUNKS * TQ, up_image.shape[2]), BF16),
            ],
        )(place, *pieces, up_image[0], down_image[0], up_text[0], down_text[0])
        return h1, exchanged(partial)

    q_image, q_text, kv_first, kv_text_first, own_rows = call(
        project_first,
        "project_first",
        [SMEM] + [VMEM] * 6,
        qkv_shapes + [row_bf16],
        rows_scratch,
        60,
    )(
        place,
        hidden_image.reshape(CHUNKS, PT, d_model),
        hidden_text.reshape(CHUNKS, TQ, d_model),
        *mods,
        *weights,
    )
    h1, received = rest_of_layer(q_image, q_text, kv_first, own_rows)
    (y_first,) = call(after_mlp, "after_mlp", [SMEM] + [VMEM] * 8, [row_bf16])(
        place, h1, *received, *mods
    )
    arrived = to_next_section(y_first, 0)
    pieces = spread_z(jnp.stack([arrived, to_next_section(y_first, 1)]))
    q_image, q_text, kv_next, kv_text_next = call(
        project_next, "project_next", [SMEM] + [VMEM] * 8, qkv_shapes, rows_scratch
    )(place, *pieces, *mods, *weights)
    h1, received = rest_of_layer(q_image, q_text, kv_next, arrived)
    tail = ((TQ, d_model + PT * channels // TQ), BF16)
    (tail_rows,) = call(last_rows, "last_rows", [SMEM] + [VMEM] * 11, [tail])(
        place, h1, *received, *mods, mod_final, jnp.transpose(final_weight), y_first
    )
    shared = lax.all_to_all(
        jnp.broadcast_to(tail_rows[None], (2 * CHUNKS,) + tail_rows.shape),
        ("section", "tp"),
        0,
        0,
        tiled=True,
    )
    index_value = timestep.astype(F32)
    sigma_now = sigma_of(index_value)
    sigma_next = sigma_of(index_value + 1.0)
    factor = jnp.where(section == 0, sigma_next - sigma_now, -sigma_now)
    latent_part, text_hidden = call(
        outputs,
        "outputs",
        [SMEM] * 2 + [VMEM] * 2,
        [((REQ, channels, span), F32), ((CHUNKS, TQ, d_model), BF16)],
    )(place, factor, shared, jnp.transpose(latent, (0, 2, 1)))
    image_kv = jnp.where(section == 0, kv_first[:, : 2 * width], kv_next[:, : 2 * width])
    text_kv = jnp.where(section == 0, kv_text_first, kv_text_next)
    return (
        jnp.transpose(latent_part, (0, 2, 1))[None],
        jnp.transpose(image_kv.reshape(REQ, 2, width, span), (0, 3, 1, 2))[None],
        text_kv.reshape(1, REQ, count, 2, width),
        text_hidden.reshape(1, REQ, count, d_model),
    )


def solution(mesh):
    in_specs = (
        P(None, "seq", None),
        P(None, "seq", None),
        P(None, "seq", None),
        P(),
        P(),
        P(),
        P(),
        P("section", None, "seq", None, "tp"),
        P("section", None, "seq", None, "tp"),
        P("section", None, None, None),
        P("section", None, None, None),
        P(),
        P("section", None, None, "tp"),
        P("section", "tp", None),
        P("section", None, "tp"),
        P("section", "tp", None),
        P("section", None, None, "tp"),
        P("section", "tp", None),
        P("section", None, "tp"),
        P("section", "tp", None),
        P(),
    )
    out_specs = (
        P("section", None, "seq", None),
        P("section", None, "seq", None, "tp"),
        P("section", None, "seq", None, "tp"),
        P("section", None, "seq", None),
    )
    return jax.shard_map(
        on_device, mesh=mesh, in_specs=in_specs, out_specs=out_specs, check_vma=False
    )
```

```python
import jax
import jax.numpy as jnp
from jax import lax
from jax.experimental import pallas as pl
from jax.experimental.pallas import tpu as pltpu
from jax.sharding import PartitionSpec as P

HD = 64
STEPS = 28
EPSILON = 1e-06
NEGATIVE = -1e30
TIME_SHIFT = 3.0

F32 = jnp.float32
BF16 = jnp.bfloat16

REQ, SLOTS, PT, TQ = 2, 4, 32, 8
ROWS = PT + TQ
CHUNKS = REQ * SLOTS
Z, X = 4, 2
Y, C = 4, 2
LANES = 128
RING = (2, 1, 3)
PIECES = ((0, 0), (0, 1), (1, 0), (1, 1), (3, 0), (3, 1), (2, 0), (2, 1))

VMEM = pl.BlockSpec(memory_space=pltpu.VMEM)
SMEM = pl.BlockSpec(memory_space=pltpu.SMEM)


def call(body, name, in_specs, out_shapes, scratch=(), mib=40):
    return pl.pallas_call(
        body,
        name=name,
        in_specs=list(in_specs),
        out_specs=[VMEM] * len(out_shapes),
        out_shape=[jax.ShapeDtypeStruct(*each) for each in out_shapes],
        scratch_shapes=list(scratch),
        compiler_params=pltpu.CompilerParams(vmem_limit_bytes=mib * 1024 * 1024),
    )


def along_z(value, step):
    pairs = [(z * X + x, (z + step) % Z * X + x) for z in range(Z) for x in range(X)]
    return lax.ppermute(value, "tp", pairs)


def across_x(value):
    return lax.ppermute(value, "tp", [(i, i ^ 1) for i in range(Z * X)])


def along_y(value, step):
    pairs = [(y * C + c, (y + step) % Y * C + c) for y in range(Y) for c in range(C)]
    return lax.ppermute(value, "seq", pairs)


def across_core(value):
    return lax.ppermute(value, "seq", [(i, i ^ 1) for i in range(Y * C)])


def to_next_section(value, flip):
    size = Z * X
    return lax.ppermute(value, ("section", "tp"), [(i, size + (i ^ flip)) for i in range(size)])


def gathered_seq(value):
    far = {(0, 0): value, (0, 1): across_core(value)}
    for step in RING:
        far[step, 0] = along_y(value, step)
    for step in RING:
        far[step, 1] = across_core(far[step, 0])
    return [far[piece] for piece in PIECES]


def spread_z(pair):
    received = {step: along_z(pair, step) for step in RING}
    return [pair] + [received[step] for step in (1, 2, 3)]


def normed(rows, shift, scale):
    mean_value = jnp.mean(rows, axis=-1, keepdims=True)
    centred = rows - mean_value
    variance = jnp.mean(centred * centred, axis=-1, keepdims=True)
    return centred * lax.rsqrt(variance + EPSILON) * (1.0 + scale) + shift


def mm(left, right):
    return jnp.dot(left, right, preferred_element_type=F32)


def mm_t(left, right):
    return lax.dot_general(left, right, (((1,), (1,)), ((), ())), preferred_element_type=F32)


def project_all(image_rows, text_rows, w_image, w_text, q_image, q_text, kv, kv_text):
    width = q_image.shape[1]
    image = image_rows[...]
    text = text_rows[...].astype(BF16)
    q_image[...] = mm_t(image, w_image[0:width, :]).astype(BF16)
    q_text[...] = mm_t(text, w_text[0:width, :]).astype(BF16).astype(F32)
    keys_values = mm_t(w_image[width:, :], image).astype(BF16)
    text_kv = mm_t(text, w_text[width:, :]).astype(BF16)
    kv_text[...] = text_kv
    span, count = SLOTS * PT, SLOTS * TQ
    for r in range(REQ):
        kv[r, 0 : 2 * width, :] = keys_values[:, r * span : (r + 1) * span]
        for i in range(2 * width // LANES):
            at = 2 * width + i * count
            kv[r, at : at + count, :] = text_kv[
                r * count : (r + 1) * count, i * LANES : (i + 1) * LANES
            ]


def project_first(place, image, text, mod_image, mod_text, *refs):
    weights, outs, own, (image_rows, text_rows) = refs[:2], refs[2:6], refs[6], refs[7:]
    tp = place[2]
    own[0:PT, :] = image[tp]
    own[PT:ROWS, :] = text[tp]
    for r in range(REQ):
        span, count = SLOTS * PT, SLOTS * TQ
        rows = image[r * SLOTS : (r + 1) * SLOTS].astype(F32).reshape(span, image.shape[2])
        image_rows[r * span : (r + 1) * span, :] = normed(
            rows, mod_image[0, r : r + 1], mod_image[1, r : r + 1]
        ).astype(BF16)
        rows = text[r * SLOTS : (r + 1) * SLOTS].astype(F32).reshape(count, text.shape[2])
        text_rows[r * count : (r + 1) * count, :] = normed(
            rows, mod_text[0, r : r + 1], mod_text[1, r : r + 1]
        )
    project_all(image_rows, text_rows, *weights, *outs)


def chunk_at(place, step, flip):
    return (place[0] + Z - step) % Z * X + (place[1] + flip) % X


def project_next(place, p0, p1, p2, p3, mod_image, mod_text, *refs):
    weights, outs, (image_rows, text_rows) = refs[:2], refs[2:6], refs[6:]
    for step, piece in enumerate((p0, p1, p2, p3)):
        for flip in range(X):
            chunk = chunk_at(place, step, flip)
            r = chunk // SLOTS
            image_rows[pl.ds(pl.multiple_of(chunk * PT, PT), PT), :] = normed(
                piece[flip, 0:PT, :].astype(F32),
                mod_image[0, pl.ds(r, 1), :],
                mod_image[1, pl.ds(r, 1), :],
            ).astype(BF16)
            text_rows[pl.ds(pl.multiple_of(chunk * TQ, TQ), TQ), :] = normed(
                piece[flip, PT:ROWS, :].astype(F32),
                mod_text[0, pl.ds(r, 1), :],
                mod_text[1, pl.ds(r, 1), :],
            )
    project_all(image_rows, text_rows, *weights, *outs)


def slot_of(patch, order):
    return sum(jnp.where(patch == order[k], k, 0) for k in range(SLOTS))


def attend(place, order, bias, q_image, q_text, *refs):
    fresh, stale = refs[0:8], refs[8:16]
    out_image, out_text = refs[16:18]
    outs, (o_image, o_text, image, text) = refs[18:26], refs[26:]
    width = q_image.shape[1]
    heads = width // HD
    span, count = SLOTS * PT, SLOTS * TQ
    rows = span + count
    image_keys = len(fresh) * span
    key_count = image_keys + len(fresh) * count
    lane_head = lax.broadcasted_iota(jnp.int32, (rows, width), 1) // HD
    row = lax.broadcasted_iota(jnp.int32, (heads * rows, 1), 0) % rows
    row_slot = jnp.where(row < span, slot_of(row // PT, order), (row - span) // TQ)
    key = lax.broadcasted_iota(jnp.int32, (1, key_count), 1)
    key_slot = jnp.where(
        key < image_keys, slot_of(key % span // PT, order), (key - image_keys) % count // TQ
    )
    is_fresh = key_slot <= row_slot

    def text_of(pieces, r):
        return jnp.concatenate(
            [
                jnp.concatenate(
                    [
                        piece[r, 2 * width + i * count : 2 * width + (i + 1) * count, :]
                        for i in range(2 * width // LANES)
                    ],
                    axis=1,
                )
                for piece in pieces
            ],
            axis=0,
        )

    fresh_share = jnp.where(is_fresh, 1.0, 0.0).astype(BF16)

    def all_of(pieces, r, at):
        return jnp.concatenate([piece[r, at : at + width, :] for piece in pieces], axis=1)

    for r in range(REQ):
        q = jnp.concatenate(
            [
                q_image[r * span : (r + 1) * span, :].astype(F32),
                q_text[r * count : (r + 1) * count, :],
            ],
            axis=0,
        )
        q = q * HD ** (-0.5)
        queries = jnp.concatenate(
            [jnp.where(lane_head == h, q, 0.0) for h in range(heads)], axis=0
        ).astype(BF16)
        fresh_text, stale_text = text_of(fresh, r), text_of(stale, r)
        image_scores = jnp.where(
            is_fresh[:, 0:image_keys],
            mm(queries, all_of(fresh, r, 0)),
            mm(queries, all_of(stale, r, 0)),
        )
        text_scores = jnp.where(
            is_fresh[:, image_keys:],
            mm_t(queries, fresh_text[:, 0:width]),
            mm_t(queries, stale_text[:, 0:width]),
        ) + bias[r : r + 1, image_keys:]
        top = jnp.maximum(
            jnp.max(image_scores, axis=-1, keepdims=True),
            jnp.max(text_scores, axis=-1, keepdims=True),
        )
        image_weights = jnp.exp(image_scores - top)
        text_weights = jnp.exp(text_scores - top)
        total = jnp.sum(image_weights, axis=-1, keepdims=True) + jnp.sum(
            text_weights, axis=-1, keepdims=True
        )
        whole = image_weights.astype(BF16)
        part = whole * fresh_share[:, 0:image_keys]
        summed = mm_t(part, all_of(fresh, r, width)) + mm_t(
            whole - part, all_of(stale, r, width)
        )
        whole = text_weights.astype(BF16)
        part = whole * fresh_share[:, image_keys:]
        summed = (
            summed
            + mm(part, fresh_text[:, width:])
            + mm(whole - part, stale_text[:, width:])
        )
        summed = summed / total
        merged = summed[0:rows]
        for h in range(1, heads):
            merged = jnp.where(lane_head == h, summed[h * rows : (h + 1) * rows], merged)
        o_image[r * span : (r + 1) * span, :] = merged[0:span].astype(BF16)
        o_text[r * count : (r + 1) * count, :] = merged[span:].astype(BF16)
    image[...] = mm(o_image[...], out_image[...])
    text[...] = mm(o_text[...], out_text[...])
    for i, out in enumerate(outs):
        chunk = (place[0] + i // X) % Z * X + (place[1] + i % X) % X
        out[0:PT, :] = image[pl.ds(pl.multiple_of(chunk * PT, PT), PT), :].astype(BF16)
        out[PT:ROWS, :] = text[pl.ds(pl.multiple_of(chunk * TQ, TQ), TQ), :].astype(BF16)


def add_far(p0, p1, p2, p3, out):
    out[...] = summed_parts((p0, p1, p2, p3)).astype(BF16)


def pack_stale(image, text, out):
    width = image.shape[1]
    count = SLOTS * TQ
    for r in range(REQ):
        out[r, 0:width, :] = image[r]
        for i in range(width // LANES):
            out[r, width + i * count : width + (i + 1) * count, :] = text[
                r, :, i * LANES : (i + 1) * LANES
            ]


def own_mod(mod, i, place):
    return mod[i, pl.ds(place[2] // SLOTS, 1), :]


def summed_parts(parts):
    total = parts[0][...].astype(F32)
    for part in parts[1:]:
        total = total + part[...].astype(F32)
    return total


def after_attention(place, rows, p0, p1, p2, p3, p4, mod_image, mod_text, h1, b):
    summed = summed_parts((p0, p1, p2, p3, p4))
    for low, high, mod in ((0, PT, mod_image), (PT, ROWS, mod_text)):
        first = rows[low:high, :].astype(F32) + own_mod(mod, 2, place) * summed[low:high]
        h1[low:high, :] = first
        b[low:high, :] = normed(
            first, own_mod(mod, 3, place), own_mod(mod, 4, place)
        ).astype(BF16)


def feed_forward(place, p0, p1, p2, p3, up_image, down_image, up_text, down_text, *refs):
    outs, (image_rows, text_rows, image_hidden, text_hidden) = refs[:8], refs[8:]
    for d, piece in enumerate((p0, p1, p2, p3)):
        for flip in range(X):
            at = d * X + flip
            image_rows[at * PT : (at + 1) * PT, :] = piece[flip, 0:PT, :]
            text_rows[at * TQ : (at + 1) * TQ, :] = piece[flip, PT:ROWS, :].astype(F32)
    hidden_width, d_model = down_image.shape
    block = hidden_width // 3

    @pl.loop(0, hidden_width // block)
    def _(j):
        lanes = pl.ds(pl.multiple_of(j * block, block), block)
        for rows, up, hidden in (
            (image_rows, up_image, image_hidden),
            (text_rows, up_text, text_hidden),
        ):
            hidden[:, lanes] = jax.nn.gelu(
                mm(rows[...].astype(BF16), up[:, lanes]), approximate=True
            ).astype(BF16)

    wide = d_model // 3

    @pl.loop(0, d_model // wide)
    def _(j):
        lanes = pl.ds(pl.multiple_of(j * wide, wide), wide)
        image = mm(image_hidden[...], down_image[:, lanes])
        text = mm(text_hidden[...], down_text[:, lanes])
        for d in range(Z):
            for flip in range(X):
                at = d * X + flip
                out = outs[(Z - d) % Z * X + flip]
                out[0:PT, lanes] = image[at * PT : (at + 1) * PT].astype(BF16)
                out[PT:ROWS, lanes] = text[at * TQ : (at + 1) * TQ].astype(BF16)


def layer_rows(place, h1, parts, mod_image, mod_text):
    summed = summed_parts(parts)
    image = (h1[0:PT, :] + own_mod(mod_image, 5, place) * summed[0:PT]).astype(BF16)
    text = (h1[PT:ROWS, :] + own_mod(mod_text, 5, place) * summed[PT:ROWS]).astype(BF16)
    return image, text


def after_mlp(place, h1, p0, p1, p2, p3, p4, mod_image, mod_text, y):
    image, text = layer_rows(place, h1, (p0, p1, p2, p3, p4), mod_image, mod_text)
    y[0:PT, :] = image
    y[PT:ROWS, :] = text


def last_rows(place, h1, p0, p1, p2, p3, p4, mod_image, mod_text, mod_final, *refs):
    weight, first, out = refs
    image, text = layer_rows(place, h1, (p0, p1, p2, p3, p4), mod_image, mod_text)
    r = place[2] // SLOTS
    rows = normed(
        image.astype(F32), mod_final[pl.ds(r, 1), 0, :], mod_final[pl.ds(r, 1), 1, :]
    ).astype(BF16)
    velocity = mm_t(weight[...], rows)
    width = text.shape[-1]
    text = jnp.where(place[3] == 0, first[PT:ROWS, :].astype(F32), text.astype(F32))
    out[:, 0:width] = text.astype(BF16)
    out[:, width:] = jnp.concatenate(
        [velocity[i * TQ : (i + 1) * TQ] for i in range(velocity.shape[0] // TQ)], axis=1
    ).astype(BF16)


def outputs(place, factor, received, latent, latent_out, text_out):
    width = text_out.shape[-1]
    count = place[3] * CHUNKS
    for chunk in range(CHUNKS):
        text_out[chunk] = received[count + chunk, :, 0:width]
    for r in range(REQ):
        rows = [
            received[CHUNKS + r * SLOTS + p, :, width:].astype(F32) for p in range(SLOTS)
        ]
        for i in range(latent.shape[1] // TQ):
            velocity = jnp.concatenate([each[:, i * PT : (i + 1) * PT] for each in rows], axis=1)
            at = slice(i * TQ, (i + 1) * TQ)
            latent_out[r, at, :] = latent[r, at, :] + factor[r] * velocity


def sigma_of(index_value):
    progress = 1.0 - index_value / STEPS
    return TIME_SHIFT * progress / (1.0 + (TIME_SHIFT - 1.0) * progress)


def on_device(
    hidden_image,
    hidden_text,
    latent,
    timestep,
    text_length,
    text_keep,
    patch_order,
    stale_image_kv,
    stale_text_kv,
    mod_image,
    mod_text,
    mod_final,
    qkv_image,
    out_image,
    up_image,
    down_image,
    qkv_text,
    out_text,
    up_text,
    down_text,
    final_weight,
):
    d_model = hidden_image.shape[2]
    width = qkv_image.shape[3]
    channels = latent.shape[2]
    section = lax.axis_index("section")
    tp = lax.axis_index("tp")
    seq = lax.axis_index("seq")
    place = jnp.stack([tp // X, tp % X, tp, section]).astype(jnp.int32)
    span, count = SLOTS * PT, SLOTS * TQ
    packed_rows = 2 * width + count * 2 * width // LANES
    packed = ((REQ, packed_rows, LANES), BF16)

    stale_image = jnp.transpose(stale_image_kv[0], (0, 2, 3, 1)).reshape(REQ, 2 * width, span)
    stale_text = stale_text_kv[0].reshape(REQ, count, 2 * width)
    (stale,) = call(pack_stale, "pack_stale", [VMEM] * 2, [packed])(stale_image, stale_text)
    stale_pieces = gathered_seq(stale)

    positions = jnp.arange(text_keep.shape[1], dtype=jnp.int32)
    valid = (positions[None, :] < text_length[:, None]) & (text_keep == 1)
    text_bias = jnp.where(valid, 0.0, NEGATIVE).astype(F32).reshape(REQ, Y * C, count)
    piece_seq = [(seq // C + Y - step) % Y * C + (seq + flip) % C for step, flip in PIECES]
    text_bias = jnp.concatenate(
        [lax.dynamic_index_in_dim(text_bias, each, 1, keepdims=False) for each in piece_seq], axis=1
    )
    bias = jnp.concatenate([jnp.zeros((REQ, Y * C * span), F32), text_bias], axis=1)

    def flat_qkv(weight):
        return jnp.transpose(weight[0], (1, 2, 0)).reshape(3 * width, d_model)

    weights = flat_qkv(qkv_image), flat_qkv(qkv_text)
    mods = jnp.transpose(mod_image[0], (1, 0, 2)), jnp.transpose(mod_text[0], (1, 0, 2))

    qkv_shapes = [
        ((CHUNKS * PT, width), BF16),
        ((CHUNKS * TQ, width), F32),
        packed,
        ((CHUNKS * TQ, 2 * width), BF16),
    ]
    rows_scratch = [
        pltpu.VMEM((CHUNKS * PT, d_model), BF16),
        pltpu.VMEM((CHUNKS * TQ, d_model), F32),
    ]
    row_f32, row_bf16 = ((ROWS, d_model), F32), ((ROWS, d_model), BF16)

    def exchanged(parts):
        far = [along_z(parts[step * X + 1], step) for step in RING]
        near = [along_z(parts[step * X], step) for step in RING]
        (half,) = call(add_far, "add_far", [VMEM] * 4, [row_bf16])(parts[1], *far)
        return [parts[0], *near, across_x(half)]

    def rest_of_layer(q_image, q_text, kv, rows):
        partial = call(
            attend,
            "attend",
            [SMEM] * 2 + [VMEM] * 21,
            [row_bf16] * 8,
            [
                pltpu.VMEM((CHUNKS * PT, width), BF16),
                pltpu.VMEM((CHUNKS * TQ, width), BF16),
                pltpu.VMEM((CHUNKS * PT, d_model), F32),
                pltpu.VMEM((CHUNKS * TQ, d_model), F32),
            ],
        )(
            place,
            patch_order,
            bias,
            q_image,
            q_text,
            *gathered_seq(kv),
            *stale_pieces,
            out_image[0],
            out_text[0],
        )
        h1, b = call(
            after_attention, "after_attention", [SMEM] + [VMEM] * 8, [row_f32, row_bf16]
        )(place, rows, *exchanged(partial), *mods)
        pieces = spread_z(jnp.stack([b, across_x(b)]))
        partial = call(
            feed_forward,
            "feed_forward",
            [SMEM] + [VMEM] * 8,
            [row_bf16] * 8,
            rows_scratch
            + [
                pltpu.VMEM((CHUNKS * PT, up_image.shape[2]), BF16),
                pltpu.VMEM((CHUNKS * TQ, up_image.shape[2]), BF16),
            ],
        )(place, *pieces, up_image[0], down_image[0], up_text[0], down_text[0])
        return h1, exchanged(partial)

    q_image, q_text, kv_first, kv_text_first, own_rows = call(
        project_first,
        "project_first",
        [SMEM] + [VMEM] * 6,
        qkv_shapes + [row_bf16],
        rows_scratch,
        60,
    )(
        place,
        hidden_image.reshape(CHUNKS, PT, d_model),
        hidden_text.reshape(CHUNKS, TQ, d_model),
        *mods,
        *weights,
    )
    h1, received = rest_of_layer(q_image, q_text, kv_first, own_rows)
    (y_first,) = call(after_mlp, "after_mlp", [SMEM] + [VMEM] * 8, [row_bf16])(
        place, h1, *received, *mods
    )
    arrived = to_next_section(y_first, 0)
    pieces = spread_z(jnp.stack([arrived, to_next_section(y_first, 1)]))
    q_image, q_text, kv_next, kv_text_next = call(
        project_next, "project_next", [SMEM] + [VMEM] * 8, qkv_shapes, rows_scratch
    )(place, *pieces, *mods, *weights)
    h1, received = rest_of_layer(q_image, q_text, kv_next, arrived)
    tail = ((TQ, d_model + PT * channels // TQ), BF16)
    (tail_rows,) = call(last_rows, "last_rows", [SMEM] + [VMEM] * 11, [tail], mib=60)(
        place, h1, *received, *mods, mod_final, jnp.transpose(final_weight), y_first
    )
    shared = lax.all_to_all(
        jnp.broadcast_to(tail_rows[None], (2 * CHUNKS,) + tail_rows.shape),
        ("section", "tp"),
        0,
        0,
        tiled=True,
    )
    index_value = timestep.astype(F32)
    sigma_now = sigma_of(index_value)
    sigma_next = sigma_of(index_value + 1.0)
    factor = jnp.where(section == 0, sigma_next - sigma_now, -sigma_now)
    latent_part, text_hidden = call(
        outputs,
        "outputs",
        [SMEM] * 2 + [VMEM] * 2,
        [((REQ, channels, span), F32), ((CHUNKS, TQ, d_model), BF16)],
    )(place, factor, shared, jnp.transpose(latent, (0, 2, 1)))
    image_kv = jnp.where(section == 0, kv_first[:, : 2 * width], kv_next[:, : 2 * width])
    text_kv = jnp.where(section == 0, kv_text_first, kv_text_next)
    return (
        jnp.transpose(latent_part, (0, 2, 1))[None],
        jnp.transpose(image_kv.reshape(REQ, 2, width, span), (0, 3, 1, 2))[None],
        text_kv.reshape(1, REQ, count, 2, width),
        text_hidden.reshape(1, REQ, count, d_model),
    )


def solution(mesh):
    in_specs = (
        P(None, "seq", None),
        P(None, "seq", None),
        P(None, "seq", None),
        P(),
        P(),
        P(),
        P(),
        P("section", None, "seq", None, "tp"),
        P("section", None, "seq", None, "tp"),
        P("section", None, None, None),
        P("section", None, None, None),
        P(),
        P("section", None, None, "tp"),
        P("section", "tp", None),
        P("section", None, "tp"),
        P("section", "tp", None),
        P("section", None, None, "tp"),
        P("section", "tp", None),
        P("section", None, "tp"),
        P("section", "tp", None),
        P(),
    )
    out_specs = (
        P("section", None, "seq", None),
        P("section", None, "seq", None, "tp"),
        P("section", None, "seq", None, "tp"),
        P("section", None, "seq", None),
    )
    return jax.shard_map(
        on_device, mesh=mesh, in_specs=in_specs, out_specs=out_specs, check_vma=False
    )
```
